32 devices in a mesh: layer: 4 (over y, core), feat: 8 (over z, x).
Axes of the slice: x: 2, y: 2, z: 4, core: 2. Of those that a mesh axis runs over, the one named last changes fastest.
Arguments:
- acts: bfloat16 [4, 768, 1024], P('layer'), may hold values from -6 to 6
- targets: bfloat16 [4, 768, 1024], P('layer', 'feat'), may hold values from -6 to 6
- enc_weight: bfloat16 [4, 1024, 20480], P('layer', None, 'feat'), may hold values from -0.1875 to 0.1875
- enc_bias: float32 [4, 20480], P('layer', 'feat'), may hold values from -3 to 3
- dec_weight: bfloat16 [4, 20480, 2, 1024], P('layer', 'feat'), may hold values from -0.0390625 to 0.0390625
- dec_bias: float32 [4, 1024], P('layer'), may hold values from -3 to 3
Outputs:
- errors: float32 [4, 768, 1024], P('layer', 'feat')
- enc_grad: bfloat16 [4, 1024, 20480], P('layer', None, 'feat')
The draws below stay inside these ranges and needn't reach their ends.
All inputs are finite; a program needn't handle non-finite values.
Results may differ from the reference program's by a relative error of at most 0.006.
Values may be sent and summed in bfloat16 or wider, within the bound.
A program may use at most 128 MiB of HBM per device.

```python
import jax
import jax.numpy as jnp
from jax import lax

D = 1024
F = 20480
TOK = 768
LAYERS = 4


def block_levels(stream_key, extent, pieces, low, high):
    def one(axis_at, blocks):
        heights = jax.random.uniform(jax.random.fold_in(jax.random.fold_in(stream_key, 6), axis_at), (blocks,), jnp.float32, low / len(pieces), high / len(pieces))
        return jnp.repeat(jnp.exp(heights), extent[axis_at] // blocks).reshape((-1,) + (1,) * (len(extent) - axis_at - 1))

    gain = one(*pieces[0])
    for cut in pieces[1:]:
        gain = gain * one(*cut)
    return gain


def gaussian(key, dims, width, bound, pieces=(), kind=jnp.bfloat16):
    array = width * jax.random.normal(key, dims, jnp.float32)
    if pieces:
        array = array * block_levels(key, dims, pieces, -0.22, 0.18)
    return jnp.clip(array, -bound, bound).astype(kind)


def setup_inputs(seed: int = 0) -> dict:
    arg_keys = jax.random.split(jax.random.key(seed), 7)
    acts = gaussian(arg_keys[0], (LAYERS, TOK, D), 1.0, 6.0, ((0, 4),))
    targets = gaussian(arg_keys[1], (LAYERS, TOK, D), 1.0, 6.0, ((0, 4), (1, 8)))
    enc_weight = gaussian(arg_keys[2], (LAYERS, D, F), D ** -0.5, 0.1875, ((0, 4), (2, 8)))
    enc_bias = gaussian(arg_keys[3], (LAYERS, F), 0.5, 3.0, ((0, 4), (1, 8)), jnp.float32)
    dec_weight = gaussian(arg_keys[4], (LAYERS, F, 2, D), F ** -0.5, 0.0390625, ((0, 4), (1, 8)))
    dec_bias = gaussian(arg_keys[5], (LAYERS, D), 0.5, 3.0, ((0, 4),), jnp.float32)
    return {"acts": acts, "targets": targets, "enc_weight": enc_weight, "enc_bias": enc_bias, "dec_weight": dec_weight, "dec_bias": dec_bias}


def forward_layer(item):
    inputs, weight, bias, decoder = item
    pre = jnp.dot(inputs, weight, preferred_element_type=jnp.float32) + bias
    latent = (jax.nn.softplus(4.0 * pre) * 0.25).astype(jnp.bfloat16)
    own = jnp.dot(latent, decoder[:, 0, :], preferred_element_type=jnp.float32)
    later = jnp.dot(latent, decoder[:, 1, :], preferred_element_type=jnp.float32)
    return pre, own, later


def reference(acts, targets, enc_weight, enc_bias, dec_weight, dec_bias):
    pres, owns, laters = lax.map(forward_layer, (acts, enc_weight, enc_bias, dec_weight))
    carried = jnp.concatenate([jnp.zeros_like(laters[:1]), laters[:-1]], axis=0)
    errors = owns + carried + dec_bias[:, None, :] - targets.astype(jnp.float32)
    err_half = errors.astype(jnp.bfloat16)
    following = jnp.concatenate([err_half[1:], jnp.zeros_like(err_half[:1])], axis=0)
    scale = acts.shape[1] ** -0.5

    def backward_layer(item):
        inputs, pre, decoder, first, second = item
        grad_latent = lax.dot_general(first, decoder[:, 0, :], (((1,), (1,)), ((), ())), preferred_element_type=jnp.float32)
        grad_latent = grad_latent + lax.dot_general(second, decoder[:, 1, :], (((1,), (1,)), ((), ())), preferred_element_type=jnp.float32)
        grad_pre = (grad_latent * jax.nn.sigmoid(4.0 * pre)).astype(jnp.bfloat16)
        total = lax.dot_general(inputs, grad_pre, (((0,), (0,)), ((), ())), preferred_element_type=jnp.float32)
        return (total * scale).astype(jnp.bfloat16)

    enc_grad = lax.map(backward_layer, (acts, pres, dec_weight, err_half, following))
    return errors, enc_grad
```

```python
import functools

import jax
import jax.numpy as jnp
from jax import lax
from jax.experimental import pallas as pl
from jax.experimental.pallas import tpu as pltpu
from jax.sharding import PartitionSpec as P

MESH = pl.DeviceIdType.MESH
PIECES = 2


def inner_of(n):
    return max(d for d in range(1, n + 1) if n % d == 0 and d * d <= n)


def chunks_of(rows):
    return next((c for c in (3, 2) if rows % (16 * c) == 0), 1)


def tile_of(features):
    return features // 2 if features % 256 == 0 else features


def contract_width(errs, decoder):
    return lax.dot_general(
        errs, decoder, (((1,), (1,)), ((), ())), preferred_element_type=jnp.float32
    )


def step_kernel(
    layers, m, o, acts_hbm, enc_hbm, dec_hbm, enc_bias_ref, targets_ref, bias_ref,
    errors_ref, grad_ref, acts,
    enc, raw, dec, deriv, latent, own, later, arrived, sums, near, mids, far, gath, foll,
    acts_sem, enc_sem, dec_sem, up_send, up_recv, near_send, near_recv, far_send, far_recv,
    out_send, out_recv, in_send, in_recv, down_send, down_recv,
):
    layer = lax.axis_index("layer")
    me = lax.axis_index("feat")
    z, x = me // m, lax.rem(me, m)
    above = lax.rem(layer + 1, layers)
    below = lax.rem(layer + layers - 1, layers)
    chunks, block, width = later.shape
    rows = block // (m * o)
    features = enc.shape[1]
    tile = tile_of(features)
    tiles = features // tile
    raws = raw.shape[0] // dec_sem.shape[0]
    wide = width // PIECES

    def at(zz, xx):
        return lax.rem(zz, o) * m + lax.rem(xx, m)

    def cols(h):
        return pl.ds(pl.multiple_of(h * wide, wide), wide)

    def feats(t):
        return pl.ds(pl.multiple_of(t * tile, tile), tile)

    def remote(src, dst, send, recv, where):
        return pltpu.make_async_remote_copy(
            src_ref=src, dst_ref=dst, send_sem=send, recv_sem=recv,
            device_id=where, device_id_type=MESH,
        )

    def load_acts(c, q):
        return pltpu.make_async_copy(acts_hbm.at[:, q, c], acts.at[c, q], acts_sem.at[c, q])

    def load_enc(t):
        return pltpu.make_async_copy(enc_hbm.at[:, feats(t)], enc.at[:, feats(t)], enc_sem.at[t])

    def load_dec(i):
        part = pl.ds(pl.multiple_of(i * raws, raws), raws)
        return pltpu.make_async_copy(dec_hbm.at[part], raw.at[part], dec_sem.at[i])

    def up(c, h):
        return remote(
            later.at[c, :, cols(h)], arrived.at[c, :, cols(h)],
            up_send.at[c, h], up_recv.at[c, h], (above, me),
        )

    def add_near(c, h, q):
        to = lax.rem(x + q, m)
        return remote(
            sums.at[c, to, :, :, cols(h)], near.at[c, q - 1, :, :, cols(h)],
            near_send.at[c, h, q - 1], near_recv.at[c, h, q - 1], (layer, at(z, to)),
        )

    def add_far(c, h, r):
        to = lax.rem(z + r, o)
        return remote(
            mids.at[c, to, :, cols(h)], far.at[c, r - 1, :, cols(h)],
            far_send.at[c, h, r - 1], far_recv.at[c, h, r - 1], (layer, at(to, x)),
        )

    def give_far(c, h, r, owner):
        spot = gath.at[c, x, owner, :, cols(h)]
        return remote(spot, spot, out_send.at[c, h, r - 1], out_recv.at[c, h, r - 1], (layer, at(z + r, x)))

    def give_near(c, h, q, column):
        spot = gath.at[c, column, :, :, cols(h)]
        return remote(spot, spot, in_send.at[c, h, q - 1], in_recv.at[c, h, q - 1], (layer, at(z, x + q)))

    def down(c, h, q):
        column = lax.rem(x + m - q, m)
        return remote(
            gath.at[c, column, :, :, cols(h)], foll.at[c, column, :, :, cols(h)],
            down_send.at[c, h, q], down_recv.at[c, h, q], (below, me),
        )

    def encode(c, t):
        lhs = acts[c].reshape(block, width)
        pre = jnp.dot(lhs, enc[:, feats(t)], preferred_element_type=jnp.float32)
        scaled = 4.0 * (pre + enc_bias_ref[:, feats(t)])
        shrunk = jnp.exp(-jnp.abs(scaled))
        latent[:, feats(t)] = ((jnp.maximum(scaled, 0.0) + jnp.log1p(shrunk)) * 0.25).astype(jnp.bfloat16)
        part = 1.0 / (1.0 + shrunk)
        deriv[c, :, feats(t)] = jnp.where(scaled >= 0.0, part, shrunk * part)

    def decode_later(c, h):
        later[c, :, cols(h)] = jnp.dot(
            latent[...], dec[1, :, cols(h)], preferred_element_type=jnp.float32
        ).astype(jnp.bfloat16)

        @pl.when(layer < layers - 1)
        def _():
            up(c, h).start()

    def decode_own(c, h):
        own[lax.rem(c, 2), :, cols(h)] = jnp.dot(latent[...], dec[0, :, cols(h)], preferred_element_type=jnp.float32)

    def send_near(c, h):
        @pl.when(layer > 0)
        def _():
            up(c, h).wait_recv()

        carried = jnp.where(layer > 0, arrived[c, :, cols(h)].astype(jnp.float32), 0.0)
        total = (own[lax.rem(c, 2), :, cols(h)] + carried).astype(jnp.bfloat16)
        sums[c, :, :, :, cols(h)] = total.reshape(m, o, rows, wide)
        for q in range(1, m):
            add_near(c, h, q).start()

    def send_far(c, h):
        total = sums[c, x, :, :, cols(h)].astype(jnp.float32)
        for q in range(1, m):
            add_near(c, h, q).wait_recv()
            total = total + near[c, q - 1, :, :, cols(h)].astype(jnp.float32)
        mids[c, :, :, cols(h)] = total.astype(jnp.bfloat16)
        for r in range(1, o):
            add_far(c, h, r).start()

    def give(c, h):
        total = sums[c, x, z, :, cols(h)].astype(jnp.float32)
        for q in range(1, m):
            total = total + near[c, q - 1, z, :, cols(h)].astype(jnp.float32)
        for r in range(1, o):
            add_far(c, h, r).wait_recv()
            total = total + far[c, r - 1, :, cols(h)].astype(jnp.float32)
        errors = total + bias_ref[:, cols(h)] - targets_ref[c, :, cols(h)].astype(jnp.float32)
        errors_ref[c, :, cols(h)] = errors
        gath[c, x, z, :, cols(h)] = errors.astype(jnp.bfloat16)
        for r in range(1, o):
            give_far(c, h, r, z).start()

    def pass_near(c, h):
        for r in range(1, o):
            give_far(c, h, r, lax.rem(z + o - r, o)).wait_recv()
        for q in range(1, m):
            give_near(c, h, q, x).start()

        @pl.when(layer > 0)
        def _():
            down(c, h, 0).start()

    def pass_down(c, h):
        for q in range(1, m):
            give_near(c, h, q, lax.rem(x + m - q, m)).wait_recv()

            @pl.when(layer > 0)
            def _():
                down(c, h, q).start()

    def gradient(c):
        @pl.when(layer < layers - 1)
        def _():
            for h in range(PIECES):
                for q in range(m):
                    down(c, h, q).wait_recv()

        @pl.loop(0, tiles)
        def _(t):
            grad = contract_width(gath[c].reshape(block, width), dec[0, feats(t), :])
            grad = grad + contract_width(foll[c].reshape(block, width), dec[1, feats(t), :])
            grad_ref[c, :, feats(t)] = (grad * deriv[c, :, feats(t)]).astype(jnp.bfloat16)

    for q in range(m):
        load_acts(0, q).start()
    for t in range(tiles):
        load_enc(t).start()
    for i in range(dec_sem.shape[0]):
        load_dec(i).start()
    for c in range(1, chunks):
        for q in range(m):
            load_acts(c, q).start()

    @pl.when(layer == layers - 1)
    def _():
        foll[...] = jnp.zeros_like(foll)

    barrier = pltpu.get_barrier_semaphore()
    for to in (
        [(layer, at(z, x + q)) for q in range(1, m)]
        + [(layer, at(z + r, x)) for r in range(1, o)]
        + [(above, me), (below, me)]
    ):
        pl.semaphore_signal(barrier, inc=1, device_id=to, device_id_type=MESH)

    for q in range(m):
        load_acts(0, q).wait()

    @pl.loop(0, tiles)
    def _(t):
        load_enc(t).wait()
        encode(0, t)

    @pl.loop(0, dec_sem.shape[0])
    def _(i):
        load_dec(i).wait()
        part = pl.ds(pl.multiple_of(i * raws, raws), raws)
        dec[:, part, :] = jnp.transpose(raw[part], (1, 0, 2))

    for c in range(1, chunks):
        for q in range(m):
            load_acts(c, q).wait()

    pl.semaphore_wait(barrier, m + o)

    @pl.loop(0, chunks)
    def _(c):
        def earlier(back, action, h):
            @pl.when(c >= back)
            def _():
                action(c - back, h)

        decode_later(c, 0)
        earlier(1, send_near, 1)
        decode_later(c, 1)
        earlier(2, give, 0)
        decode_own(c, 0)
        earlier(1, send_far, 0)
        decode_own(c, 1)

        @pl.when(c < chunks - 1)
        def _():
            for t in range(tiles):
                encode(c + 1, t)
                if t == 0:
                    send_near(c, 0)

            @pl.when(c >= 1)
            def _():
                send_far(c - 1, 1)

    last = chunks - 1
    tail = []
    for c in range(chunks):
        for h in range(PIECES):
            base = 7.0 * c + 3.1 * h
            if c == last:
                tail.append((base + 8.6, send_near, c, h))
            if (h == 0 and c == last) or (h == 1 and c >= last - 1):
                tail.append((base + 13.1, send_far, c, h))
            if h == 1 or c >= last - 1:
                tail.append((base + 17.6, give, c, h))
            tail.append((base + 22.1, pass_near, c, h))
            tail.append((base + 26.6, pass_down, c, h))
        tail.append((7.0 * c + 35.0, lambda c, h: gradient(c), c, 0))
    for _, action, c, h in sorted(tail, key=lambda e: e[0]):
        action(c, h)

    @pl.loop(0, chunks)
    def _(c):
        for h in range(PIECES):
            @pl.when(layer < layers - 1)
            def _():
                up(c, h).wait_send()

            for q in range(1, m):
                add_near(c, h, q).wait_send()
                give_near(c, h, q, x).wait_send()
            for r in range(1, o):
                add_far(c, h, r).wait_send()
                give_far(c, h, r, z).wait_send()

            @pl.when(layer > 0)
            def _():
                for q in range(m):
                    down(c, h, q).wait_send()


def step(layers, n, acts, enc, dec, enc_bias, targets, bias):
    o, m, chunks, rows, width = acts.shape
    features = enc.shape[1]
    block = n * rows
    half, full = jnp.bfloat16, jnp.float32
    vmem = pl.BlockSpec(memory_space=pltpu.VMEM)
    anywhere = pl.BlockSpec(memory_space=pl.ANY)
    dma = pltpu.SemaphoreType.DMA
    parts = features // 256 if features % 256 == 0 else 1
    pairs = [(), (m - 1,), (o - 1,), (o - 1,), (m - 1,), (m,)]
    return pl.pallas_call(
        functools.partial(step_kernel, layers, m, o),
        out_shape=(
            jax.ShapeDtypeStruct((chunks, rows, width), full),
            jax.ShapeDtypeStruct((chunks, block, features), half),
            jax.ShapeDtypeStruct((chunks, m, o, rows, width), half),
        ),
        in_specs=[anywhere, anywhere, anywhere, vmem, vmem, vmem],
        out_specs=(vmem, vmem, vmem),
        scratch_shapes=[
            pltpu.VMEM((width, features), half),
            pltpu.VMEM((features, 2, width), half),
            pltpu.VMEM((2, features, width), half),
            pltpu.VMEM((chunks, block, features), full),
            pltpu.VMEM((block, features), half),
            pltpu.VMEM((2, block, width), full),
            pltpu.VMEM((chunks, block, width), half),
            pltpu.VMEM((chunks, block, width), half),
            pltpu.VMEM((chunks, m, o, rows, width), half),
            pltpu.VMEM((chunks, m - 1, o, rows, width), half),
            pltpu.VMEM((chunks, o, rows, width), half),
            pltpu.VMEM((chunks, o - 1, rows, width), half),
            pltpu.VMEM((chunks, m, o, rows, width), half),
            pltpu.VMEM((chunks, m, o, rows, width), half),
            dma((chunks, m)),
            dma((features // tile_of(features),)),
            dma((parts,)),
            *[dma((chunks, PIECES, *p)) for p in pairs for _ in range(2)],
        ],
        compiler_params=pltpu.CompilerParams(
            collective_id=0, has_side_effects=True, vmem_limit_bytes=58 * 2**20
        ),
        name="step",
    )(acts, enc, dec, enc_bias, targets, bias)


def weigh_kernel(scale, acts_ref, grad_ref, out_ref):
    total = lax.dot_general(
        acts_ref[...], grad_ref[...], (((0,), (0,)), ((), ())), preferred_element_type=jnp.float32
    )
    out_ref[...] = (total * scale).astype(jnp.bfloat16)


def encoder_grad(acts, grad):
    tokens, features = grad.shape
    width = acts.shape[1]
    tile = 512 if features % 512 == 0 else 256
    return pl.pallas_call(
        functools.partial(weigh_kernel, tokens ** (-0.5)),
        grid=(features // tile,),
        out_shape=jax.ShapeDtypeStruct((width, features), jnp.bfloat16),
        in_specs=[
            pl.BlockSpec(memory_space=pltpu.VMEM),
            pl.BlockSpec((tokens, tile), lambda i: (0, i)),
        ],
        out_specs=pl.BlockSpec((width, tile), lambda i: (0, i)),
        compiler_params=pltpu.CompilerParams(vmem_limit_bytes=24 * 2**20),
        name="encoder_grad",
    )(acts, grad)


def local(layers, n, acts, targets, enc_weight, enc_bias, dec_weight, dec_bias):
    tokens, width = acts.shape[1:]
    m = inner_of(n)
    rows = tokens // n
    chunks = chunks_of(rows)
    errors, grad, turned = step(
        layers, n,
        acts.reshape(n // m, m, chunks, rows // chunks, width),
        enc_weight[0], dec_weight[0], enc_bias,
        targets.reshape(chunks, rows // chunks, width), dec_bias,
    )
    enc_grad = encoder_grad(turned.reshape(tokens, width), grad.reshape(tokens, -1))
    return (errors.reshape(1, rows, width), enc_grad[None])


def solution(mesh):
    return jax.shard_map(
        functools.partial(local, mesh.shape["layer"], mesh.shape["feat"]),
        mesh=mesh,
        in_specs=(
            P("layer", None, None),
            P("layer", "feat", None),
            P("layer", None, "feat"),
            P("layer", "feat"),
            P("layer", "feat", None, None),
            P("layer", None),
        ),
        out_specs=(P("layer", "feat", None), P("layer", None, "feat")),
        check_vma=False,
    )
```

```python
import functools

import jax
import jax.numpy as jnp
from jax import lax
from jax.experimental import pallas as pl
from jax.experimental.pallas import tpu as pltpu
from jax.sharding import PartitionSpec as P

MESH = pl.DeviceIdType.MESH
PIECES = 4
DOTS = 2


def inner_of(n):
    return max(d for d in range(1, n + 1) if n % d == 0 and d * d <= n)


def chunks_of(rows):
    return next((c for c in (3, 2) if rows % (16 * c) == 0), 1)


def tile_of(features):
    return features // 2 if features % 256 == 0 else features


def contract_width(errs, decoder):
    return lax.dot_general(
        errs, decoder, (((1,), (1,)), ((), ())), preferred_element_type=jnp.float32
    )


def plan(chunks):
    places = {
        "x": ((3, 0), (4, 0), (5, 0), (0, 1)), "low": ((0, 1), (1, 1), (3, 1), (4, 1)),
        "high": ((3, 1), (4, 1), (5, 1), (0, 2)), "give_high": ((5, 1), (0, 2), (2, 2), (3, 2)),
        "give_low": ((2, 2), (3, 2), (4, 2), (5, 2)), "give_x": ((4, 2), (5, 2), (5, 2), (5, 2)),
        "down": ((5, 3), (5, 3), (5, 3), (5, 3)),
    }
    points = (0.85, 1.7, 2.55, 3.4, 5.0, 6.6)
    period = 6.6
    queued = {"down": (21.4, 22.9, 24.4, 25.9)}
    inside, rest = [[] for _ in points], []
    for stage, spots in places.items():
        for h, (spot, back) in enumerate(spots):
            when = points[spot] + back * period
            inside[spot].append((when, back, stage, h))
            final = chunks - 1 if spot < 4 else chunks - 2
            for c in range(chunks):
                if c + back > final:
                    late = queued.get(stage, spots)[h] if stage in queued else when
                    rest.append((c * period + late, stage, c, h))
    for spot in inside:
        spot.sort(key=lambda e: -e[0])
    return inside, rest


def step_kernel(
    layers, m, lo, hi, scale, acts_hbm, enc_hbm, dec_hbm, enc_bias_ref, targets_ref, bias_ref,
    errors_ref, enc,
    acts, raw, dec, deriv, latent, own, total, later, arrived, sums, near, low_in, high_in, gath, foll,
    acts_sem, enc_sem, dec_sem, up_send, up_recv, x_send, x_recv, low_send, low_recv, high_send, high_recv,
    ghigh_send, ghigh_recv, glow_send, glow_recv, gx_send, gx_recv, down_send, down_recv,
):
    layer = lax.axis_index("layer")
    me = lax.axis_index("feat")
    x = lax.rem(me, m)
    zl, zh = lax.rem(me // m, lo), me // (m * lo)
    above = lax.rem(layer + 1, layers)
    below = lax.rem(layer + layers - 1, layers)
    chunks, rows, width = later.shape[0], *later.shape[4:]
    block = m * lo * hi * rows
    features = enc.shape[1]
    tile = tile_of(features)
    tiles = features // tile
    slots, raws = raw.shape[:2]
    parts = features // raws
    wide = width // PIECES
    dot = width // DOTS

    def at(h, l, xx):
        return (lax.rem(h, hi) * lo + lax.rem(l, lo)) * m + lax.rem(xx, m)

    def cols(h):
        return pl.ds(h * wide, wide)

    def dots(d):
        return pl.ds(d * dot, dot)

    def feats(t):
        return pl.ds(pl.multiple_of(t * tile, tile), tile)

    def remote(src, dst, send, recv, where):
        return pltpu.make_async_remote_copy(
            src_ref=src, dst_ref=dst, send_sem=send, recv_sem=recv,
            device_id=where, device_id_type=MESH,
        )

    def load_acts(c, q, l):
        return pltpu.make_async_copy(acts_hbm.at[:, l, q, c], acts.at[c, q, l], acts_sem.at[c, q, l])

    def load_enc(t):
        return pltpu.make_async_copy(enc_hbm.at[:, feats(t)], enc.at[:, feats(t)], enc_sem.at[t])

    def load_dec(i):
        part = pl.ds(pl.multiple_of(i * raws, raws), raws)
        return pltpu.make_async_copy(dec_hbm.at[part], raw.at[lax.rem(i, slots)], dec_sem.at[i])

    def up(c, h):
        return remote(
            later.at[c, :, :, :, :, cols(h)], arrived.at[c, :, :, :, :, cols(h)],
            up_send.at[c, h], up_recv.at[c, h], (above, me),
        )

    def add_x(c, h, q):
        to = lax.rem(x + q, m)
        return remote(
            sums.at[c, to, :, :, :, cols(h)], near.at[c, q - 1, :, :, :, cols(h)],
            x_send.at[c, h, q - 1], x_recv.at[c, h, q - 1], (layer, at(zh, zl, to)),
        )

    def add_low(c, h, q):
        to = lax.rem(zl + q, lo)
        return remote(
            later.at[c, 0, to, :, :, cols(h)], low_in.at[c, q - 1, :, :, cols(h)],
            low_send.at[c, h, q - 1], low_recv.at[c, h, q - 1], (layer, at(zh, to, x)),
        )

    def add_high(c, h, q):
        to = lax.rem(zh + q, hi)
        return remote(
            later.at[c, 0, zl, to, :, cols(h)], high_in.at[c, q - 1, :, cols(h)],
            high_send.at[c, h, q - 1], high_recv.at[c, h, q - 1], (layer, at(to, zl, x)),
        )

    def give_high(c, h, q, owner):
        spot = gath.at[c, x, zl, owner, :, cols(h)]
        return remote(
            spot, spot, ghigh_send.at[c, h, q - 1], ghigh_recv.at[c, h, q - 1], (layer, at(zh + q, zl, x))
        )

    def give_low(c, h, q, owner):
        spot = gath.at[c, x, owner, :, :, cols(h)]
        return remote(
            spot, spot, glow_send.at[c, h, q - 1], glow_recv.at[c, h, q - 1], (layer, at(zh, zl + q, x))
        )

    def give_x(c, h, q, owner):
        spot = gath.at[c, owner, :, :, :, cols(h)]
        return remote(
            spot, spot, gx_send.at[c, h, q - 1], gx_recv.at[c, h, q - 1], (layer, at(zh, zl, x + q))
        )

    def down(c, h, q):
        owner = lax.rem(x + m - q, m)
        return remote(
            gath.at[c, owner, :, :, :, cols(h)], foll.at[c, owner, :, :, :, cols(h)],
            down_send.at[c, h, q], down_recv.at[c, h, q], (below, me),
        )

    def encode(c, t):
        lhs = acts[c].reshape(block, width)
        pre = jnp.dot(lhs, enc[:, feats(t)], preferred_element_type=jnp.float32)
        scaled = 4.0 * (pre + enc_bias_ref[:, feats(t)])
        shrunk = jnp.exp(-jnp.abs(scaled))
        latent[:, feats(t)] = ((jnp.maximum(scaled, 0.0) + jnp.log1p(shrunk)) * 0.25).astype(jnp.bfloat16)
        part = 1.0 / (1.0 + shrunk)
        deriv[c, :, feats(t)] = jnp.where(scaled >= 0.0, part, shrunk * part).astype(jnp.bfloat16)

    def decode_later(c, d):
        value = jnp.dot(latent[...], dec[1, :, dots(d)], preferred_element_type=jnp.float32)
        later[c, :, :, :, :, dots(d)] = value.astype(jnp.bfloat16).reshape(m, lo, hi, rows, dot)

        @pl.when(layer < layers - 1)
        def _():
            for h in range(d * PIECES // DOTS, (d + 1) * PIECES // DOTS):
                up(c, h).start()

    def decode_own(c, d):
        own[:, dots(d)] = jnp.dot(
            latent[...], dec[0, :, dots(d)], preferred_element_type=jnp.float32
        )

    def send_x(c, h):
        @pl.when(layer > 0)
        def _():
            up(c, h).wait_recv()

        carried = jnp.where(layer > 0, arrived[c, :, :, :, :, cols(h)].reshape(block, wide).astype(jnp.float32), 0.0)
        both = (own[:, cols(h)] + carried).astype(jnp.bfloat16)
        sums[c, :, :, :, :, cols(h)] = both.reshape(m, lo, hi, rows, wide)
        for q in range(1, m):
            add_x(c, h, q).start()

    def send_low(c, h):
        value = sums[c, x, :, :, :, cols(h)].astype(jnp.float32)
        for q in range(1, m):
            add_x(c, h, q).wait_recv()
            value = value + near[c, q - 1, :, :, :, cols(h)].astype(jnp.float32)

        @pl.when(layer < layers - 1)
        def _():
            up(c, h).wait_send()

        later[c, 0, :, :, :, cols(h)] = value.astype(jnp.bfloat16)
        for q in range(1, lo):
            add_low(c, h, q).start()

    def own_low(c, h, spot):
        value = sums[c, x, zl, spot, :, cols(h)].astype(jnp.float32)
        for q in range(1, m):
            value = value + near[c, q - 1, zl, spot, :, cols(h)].astype(jnp.float32)
        for q in range(1, lo):
            value = value + low_in[c, q - 1, spot, :, cols(h)].astype(jnp.float32)
        return value

    def send_high(c, h):
        for q in range(1, lo):
            add_low(c, h, q).wait_recv()
        for q in range(1, hi):
            to = lax.rem(zh + q, hi)
            later[c, 0, zl, to, :, cols(h)] = own_low(c, h, to).astype(jnp.bfloat16)
            add_high(c, h, q).start()

    def send_errors(c, h):
        value = own_low(c, h, zh)
        for q in range(1, hi):
            add_high(c, h, q).wait_recv()
            value = value + high_in[c, q - 1, :, cols(h)].astype(jnp.float32)
        errors = value + bias_ref[:, cols(h)] - targets_ref[c, :, cols(h)].astype(jnp.float32)
        errors_ref[c, :, cols(h)] = errors
        gath[c, x, zl, zh, :, cols(h)] = errors.astype(jnp.bfloat16)
        for q in range(1, hi):
            give_high(c, h, q, zh).start()

    def pass_low(c, h):
        for q in range(1, hi):
            give_high(c, h, q, lax.rem(zh + hi - q, hi)).wait_recv()
        for q in range(1, lo):
            give_low(c, h, q, zl).start()

    def pass_x(c, h):
        for q in range(1, lo):
            give_low(c, h, q, lax.rem(zl + lo - q, lo)).wait_recv()
        for q in range(1, m):
            give_x(c, h, q, x).start()

        @pl.when(layer > 0)
        def _():
            down(c, h, 0).start()

    def pass_down(c, h):
        for q in range(1, m):
            give_x(c, h, q, lax.rem(x + m - q, m)).wait_recv()

        @pl.when(layer > 0)
        def _():
            for q in range(1, m):
                down(c, h, q).start()

    def gradient(c, t):
        if t == 0:
            @pl.when(layer < layers - 1)
            def _():
                for h in range(PIECES):
                    for q in range(m):
                        down(c, h, q).wait_recv()

        grad = contract_width(gath[c].reshape(block, width), dec[0, feats(t), :])
        grad = grad + contract_width(foll[c].reshape(block, width), dec[1, feats(t), :])
        latent[:, feats(t)] = (grad * deriv[c, :, feats(t)].astype(jnp.float32)).astype(jnp.bfloat16)

    def weigh(c, t):
        value = lax.dot_general(
            acts[c].reshape(block, width), latent[:, feats(t)], (((0,), (0,)), ((), ())),
            preferred_element_type=jnp.float32,
        )
        if c > 0:
            value = total[:, feats(t)] + value
        if c < chunks - 1:
            total[:, feats(t)] = value
        else:
            enc[:, feats(t)] = (value * scale).astype(jnp.bfloat16)

    run = {
        "x": send_x, "low": send_low, "high": send_high, "give_high": send_errors,
        "give_low": pass_low, "give_x": pass_x, "down": pass_down, "gradient": gradient, "weigh": weigh,
    }
    inside, rest = plan(chunks)

    def every(c):
        return [load_acts(c, q, l) for q in range(m) for l in range(lo)]

    for copy in every(0):
        copy.start()
    for t in range(tiles):
        load_enc(t).start()

    @pl.when(layer == layers - 1)
    def _():
        foll[...] = jnp.zeros_like(foll)

    barrier = pltpu.get_barrier_semaphore()
    for to in (
        [(layer, at(zh, zl, x + q)) for q in range(1, m)]
        + [(layer, at(zh, zl + q, x)) for q in range(1, lo)]
        + [(layer, at(zh + q, zl, x)) for q in range(1, hi)]
        + [(above, me), (below, me)]
    ):
        pl.semaphore_signal(barrier, inc=1, device_id=to, device_id_type=MESH)

    for copy in every(0):
        copy.wait()
    load_enc(0).wait()
    for i in range(slots):
        load_dec(i).start()
    for c in range(1, chunks):
        for copy in every(c):
            copy.start()

    def split_dec(i):
        load_dec(i).wait()
        dec[:, pl.ds(pl.multiple_of(i * raws, raws), raws), :] = jnp.transpose(raw[lax.rem(i, slots)], (1, 0, 2))

        @pl.when(i + slots < parts)
        def _():
            load_dec(i + slots).start()

    encode(0, 0)
    pl.loop(0, slots)(split_dec)
    for t in range(1, tiles):
        load_enc(t).wait()
        encode(0, t)
    pl.loop(slots, parts)(split_dec)

    for c in range(1, chunks):
        for copy in every(c):
            copy.wait()

    pl.semaphore_wait(barrier, m + lo + hi - 1)

    @pl.loop(0, chunks)
    def _(c):
        def attend(spot):
            for _, back, stage, h in inside[spot]:
                @pl.when(c >= back)
                def _():
                    run[stage](c - back, h)

        decode_later(c, 0)
        attend(0)
        decode_later(c, 1)
        attend(1)
        decode_own(c, 0)
        attend(2)
        decode_own(c, 1)
        attend(3)

        @pl.when(c < chunks - 1)
        def _():
            for t in range(tiles):
                encode(c + 1, t)
                if t < 2:
                    attend(4 + t)

    for c in range(chunks):
        base = 6.6 * c + 28.0
        for t in range(tiles):
            rest.append((base + 1.6 * t, "gradient", c, t))
            rest.append((base + 3.2 + 1.0 * t, "weigh", c, t))
    for _, stage, c, k in sorted(rest, key=lambda e: e[0]):
        run[stage](c, k)

    @pl.loop(0, chunks)
    def _(c):
        for h in range(PIECES):
            for q in range(1, m):
                add_x(c, h, q).wait_send()
                give_x(c, h, q, x).wait_send()
            for q in range(1, lo):
                add_low(c, h, q).wait_send()
                give_low(c, h, q, zl).wait_send()
            for q in range(1, hi):
                add_high(c, h, q).wait_send()
                give_high(c, h, q, zh).wait_send()

            @pl.when(layer > 0)
            def _():
                for q in range(m):
                    down(c, h, q).wait_send()


def step(layers, tokens, acts, enc, dec, enc_bias, targets, bias):
    hi, lo, m, chunks, rows, width = acts.shape
    features = enc.shape[1]
    block = tokens // chunks
    half, full = jnp.bfloat16, jnp.float32
    vmem = pl.BlockSpec(memory_space=pltpu.VMEM)
    anywhere = pl.BlockSpec(memory_space=pl.ANY)
    dma = pltpu.SemaphoreType.DMA
    raws = 256
    parts = features // raws
    slots = -(-parts // 2)
    pairs = [(), (m - 1,), (lo - 1,), (hi - 1,), (hi - 1,), (lo - 1,), (m - 1,), (m,)]
    return pl.pallas_call(
        functools.partial(step_kernel, layers, m, lo, hi, tokens ** (-0.5)),
        out_shape=(
            jax.ShapeDtypeStruct((chunks, rows, width), full),
            jax.ShapeDtypeStruct((width, features), half),
        ),
        in_specs=[anywhere, anywhere, anywhere, vmem, vmem, vmem],
        out_specs=(vmem, vmem),
        scratch_shapes=[
            pltpu.VMEM((chunks, m, lo, hi, rows, width), half),
            pltpu.VMEM((slots, raws, 2, width), half),
            pltpu.VMEM((2, features, width), half),
            pltpu.VMEM((chunks, block, features), half),
            pltpu.VMEM((block, features), half),
            pltpu.VMEM((block, width), full),
            pltpu.VMEM((width, features), full),
            pltpu.VMEM((chunks, m, lo, hi, rows, width), half),
            pltpu.VMEM((chunks, m, lo, hi, rows, width), half),
            pltpu.VMEM((chunks, m, lo, hi, rows, width), half),
            pltpu.VMEM((chunks, m - 1, lo, hi, rows, width), half),
            pltpu.VMEM((chunks, lo - 1, hi, rows, width), half),
            pltpu.VMEM((chunks, hi - 1, rows, width), half),
            pltpu.VMEM((chunks, m, lo, hi, rows, width), half),
            pltpu.VMEM((chunks, m, lo, hi, rows, width), half),
            dma((chunks, m, lo)),
            dma((features // tile_of(features),)),
            dma((parts,)),
            *[dma((chunks, PIECES, *p)) for p in pairs for _ in range(2)],
        ],
        compiler_params=pltpu.CompilerParams(
            collective_id=0, has_side_effects=True, vmem_limit_bytes=46 * 2**20
        ),
        name="step",
    )(acts, enc, dec, enc_bias, targets, bias)


def local(layers, n, acts, targets, enc_weight, enc_bias, dec_weight, dec_bias):
    tokens, width = acts.shape[1:]
    m = inner_of(n)
    lo = inner_of(n // m)
    rows = tokens // n
    chunks = chunks_of(rows)
    errors, enc_grad = step(
        layers, tokens,
        acts.reshape(n // (m * lo), lo, m, chunks, rows // chunks, width),
        enc_weight[0], dec_weight[0], enc_bias,
        targets.reshape(chunks, rows // chunks, width), dec_bias,
    )
    return (errors.reshape(1, rows, width), enc_grad[None])


def solution(mesh):
    return jax.shard_map(
        functools.partial(local, mesh.shape["layer"], mesh.shape["feat"]),
        mesh=mesh,
        in_specs=(
            P("layer", None, None),
            P("layer", "feat", None),
            P("layer", None, "feat"),
            P("layer", "feat"),
            P("layer", "feat", None, None),
            P("layer", None),
        ),
        out_specs=(P("layer", "feat", None), P("layer", None, "feat")),
        check_vma=False,
    )
```

```python
import functools

import jax
import jax.numpy as jnp
from jax import lax
from jax.experimental import pallas as pl
from jax.experimental.pallas import tpu as pltpu
from jax.sharding import PartitionSpec as P

MESH = pl.DeviceIdType.MESH
PIECES = 4
DOTS = 2


def inner_of(n):
    return max(d for d in range(1, n + 1) if n % d == 0 and d * d <= n)


def chunks_of(rows):
    return next((c for c in (3, 2) if rows % (16 * c) == 0), 1)


def tile_of(features):
    return features // 2 if features % 256 == 0 else features


def contract_width(errs, decoder):
    return lax.dot_general(
        errs, decoder, (((1,), (1,)), ((), ())), preferred_element_type=jnp.float32
    )


SPOTS = {
    "x": (3, 4, 6, 6),
    "low": (5, 7, 10, 10),
    "high": (8, 10, 12, 12),
    "give_z": (11, 13, 15, 15),
    "give_x": (15, 21, 23, 18),
    "down": (28, 23, 29, 24),
}
REST = {
    "x": ((0, 0, 0, 0), (0, 0, 0, 0), (0, 1, 2, 0)),
    "low": ((0, 0, 0, 0), (0, 0, 4, 3), (6, 10, 9, 20)),
    "high": ((0, 0, 0, 0), (0, 5, 7, 11), (18, 26, 25, 38)),
    "give_z": ((0, 0, 0, 0), (8, 12, 19, 27), (30, 36, 41, 47)),
    "give_x": ((0, 16, 17, 22), (33, 28, 40, 35), (55, 51, 54, 58)),
    "down": ((32, 23, 24, 31), (44, 43, 50, 49), (61, 57, 60, 63)),
    "gradient": ((34, 42), (56, 59), (65, 66)),
    "weigh": ((46, 52), (62, 64), (67, 68)),
}


def plan(chunks, tiles):
    inside, rest = [[] for _ in range(6)], []
    ends = len(REST["x"])

    def rank(stage, c, k):
        rows = REST[stage]
        return (rows[max(0, min(c, ends - 1 - (chunks - 1 - c)))][k], c)

    for stage, spots in SPOTS.items():
        for h, place in enumerate(spots):
            back, spot = divmod(place, 6)
            inside[spot].append((back, stage, h))
            final = chunks - 1 if spot < 4 else chunks - 2
            rest += [(stage, c, h) for c in range(chunks) if c + back > final]
    for spot in inside:
        spot.sort(key=lambda e: -e[0])
    rest += [(stage, c, t) for c in range(chunks) for stage in ("gradient", "weigh") for t in range(tiles)]
    return inside, sorted(rest, key=lambda e: rank(*e))


def step_kernel(
    layers, m, lo, hi, scale, acts_hbm, enc_hbm, dec_hbm, enc_bias_hbm, targets_hbm, bias_hbm,
    errors_ref, enc,
    enc_bias_ref, targets_ref, bias_ref, acts, raw, dec, deriv, latent, own, total, later, arrived, sums, near, low_in, high_in, gath, foll,
    small_sem, acts_sem, enc_sem, dec_sem, up_send, up_recv, x_send, x_recv, low_send, low_recv, high_send, high_recv,
    gz_send, gz_recv, gx_send, gx_recv, down_send, down_recv,
):
    layer = lax.axis_index("layer")
    me = lax.axis_index("feat")
    x = lax.rem(me, m)
    zl, zh = lax.rem(me // m, lo), me // (m * lo)
    above = lax.rem(layer + 1, layers)
    below = lax.rem(layer + layers - 1, layers)
    chunks, rows, width = later.shape[0], *later.shape[4:]
    block = m * lo * hi * rows
    features = enc.shape[1]
    tile = tile_of(features)
    tiles = features // tile
    slots, raws = raw.shape[:2]
    parts = features // raws
    deep, mine = lo * hi, zl * hi + zh
    wide = width // PIECES
    dot = width // DOTS

    def at(h, l, xx):
        return (lax.rem(h, hi) * lo + lax.rem(l, lo)) * m + lax.rem(xx, m)

    def cols(h):
        return pl.ds(h * wide, wide)

    def dots(d):
        return pl.ds(d * dot, dot)

    def feats(t):
        return pl.ds(pl.multiple_of(t * tile, tile), tile)

    def remote(src, dst, send, recv, where):
        return pltpu.make_async_remote_copy(
            src_ref=src, dst_ref=dst, send_sem=send, recv_sem=recv,
            device_id=where, device_id_type=MESH,
        )

    def load_acts(c, q, l):
        return pltpu.make_async_copy(acts_hbm.at[:, l, q, c], acts.at[c, q, l], acts_sem.at[c, q, l])

    def load_enc(t):
        return pltpu.make_async_copy(enc_hbm.at[:, feats(t)], enc.at[:, feats(t)], enc_sem.at[t])

    def load_dec(i):
        part = pl.ds(pl.multiple_of(i * raws, raws), raws)
        return pltpu.make_async_copy(dec_hbm.at[part], raw.at[lax.rem(i, slots)], dec_sem.at[i])

    def up(c, h):
        return remote(
            later.at[c, :, :, :, :, cols(h)], arrived.at[c, :, :, :, :, cols(h)],
            up_send.at[c, h], up_recv.at[c, h], (above, me),
        )

    def add_x(c, h, q):
        to = lax.rem(x + q, m)
        return remote(
            sums.at[c, to, :, :, :, cols(h)], near.at[c, q - 1, :, :, :, cols(h)],
            x_send.at[c, h, q - 1], x_recv.at[c, h, q - 1], (layer, at(zh, zl, to)),
        )

    def add_low(c, h, q):
        to = lax.rem(zl + q, lo)
        return remote(
            later.at[c, 0, to, :, :, cols(h)], low_in.at[c, q - 1, :, :, cols(h)],
            low_send.at[c, h, q - 1], low_recv.at[c, h, q - 1], (layer, at(zh, to, x)),
        )

    def add_high(c, h, q):
        to = lax.rem(zh + q, hi)
        return remote(
            later.at[c, 0, zl, to, :, cols(h)], high_in.at[c, q - 1, :, cols(h)],
            high_send.at[c, h, q - 1], high_recv.at[c, h, q - 1], (layer, at(to, zl, x)),
        )

    def give_z(c, h, q, owner):
        spot = gath.at[c, x, owner // hi, lax.rem(owner, hi), :, cols(h)]
        to = lax.rem(mine + q, deep)
        return remote(
            spot, spot, gz_send.at[c, h, q - 1], gz_recv.at[c, h, q - 1], (layer, at(lax.rem(to, hi), to // hi, x))
        )

    def give_x(c, h, q, owner):
        spot = gath.at[c, owner, :, :, :, cols(h)]
        return remote(
            spot, spot, gx_send.at[c, h, q - 1], gx_recv.at[c, h, q - 1], (layer, at(zh, zl, x + q))
        )

    def down(c, h, q):
        owner = lax.rem(x + m - q, m)
        return remote(
            gath.at[c, owner, :, :, :, cols(h)], foll.at[c, owner, :, :, :, cols(h)],
            down_send.at[c, h, q], down_recv.at[c, h, q], (below, me),
        )

    def encode(c, t):
        lhs = acts[c].reshape(block, width)
        pre = jnp.dot(lhs, enc[:, feats(t)], preferred_element_type=jnp.float32)
        scaled = 4.0 * (pre + enc_bias_ref[:, feats(t)])
        shrunk = jnp.exp(-jnp.abs(scaled))
        latent[:, feats(t)] = ((jnp.maximum(scaled, 0.0) + jnp.log1p(shrunk)) * 0.25).astype(jnp.bfloat16)
        part = 1.0 / (1.0 + shrunk)
        deriv[c, :, feats(t)] = jnp.where(scaled >= 0.0, part, shrunk * part).astype(jnp.bfloat16)

    def decode_later(c, d):
        value = jnp.dot(latent[...], dec[1, :, dots(d)], preferred_element_type=jnp.float32)
        later[c, :, :, :, :, dots(d)] = value.astype(jnp.bfloat16).reshape(m, lo, hi, rows, dot)

        @pl.when(layer < layers - 1)
        def _():
            for h in range(d * PIECES // DOTS, (d + 1) * PIECES // DOTS):
                up(c, h).start()

    def decode_own(c, d):
        own[:, dots(d)] = jnp.dot(
            latent[...], dec[0, :, dots(d)], preferred_element_type=jnp.float32
        )

    def send_x(c, h):
        @pl.when(layer > 0)
        def _():
            up(c, h).wait_recv()

        carried = jnp.where(layer > 0, arrived[c, :, :, :, :, cols(h)].reshape(block, wide).astype(jnp.float32), 0.0)
        both = (own[:, cols(h)] + carried).astype(jnp.bfloat16)
        sums[c, :, :, :, :, cols(h)] = both.reshape(m, lo, hi, rows, wide)
        for q in range(1, m):
            add_x(c, h, q).start()

    def send_low(c, h):
        value = sums[c, x, :, :, :, cols(h)].astype(jnp.float32)
        for q in range(1, m):
            add_x(c, h, q).wait_recv()
            value = value + near[c, q - 1, :, :, :, cols(h)].astype(jnp.float32)

        @pl.when(layer < layers - 1)
        def _():
            up(c, h).wait_send()

        later[c, 0, :, :, :, cols(h)] = value.astype(jnp.bfloat16)
        for q in range(1, lo):
            add_low(c, h, q).start()

    def own_low(c, h, spot):
        value = sums[c, x, zl, spot, :, cols(h)].astype(jnp.float32)
        for q in range(1, m):
            value = value + near[c, q - 1, zl, spot, :, cols(h)].astype(jnp.float32)
        for q in range(1, lo):
            value = value + low_in[c, q - 1, spot, :, cols(h)].astype(jnp.float32)
        return value

    def send_high(c, h):
        for q in range(1, lo):
            add_low(c, h, q).wait_recv()
        for q in range(1, hi):
            to = lax.rem(zh + q, hi)
            later[c, 0, zl, to, :, cols(h)] = own_low(c, h, to).astype(jnp.bfloat16)
            add_high(c, h, q).start()

    def send_errors(c, h):
        value = own_low(c, h, zh)
        for q in range(1, hi):
            add_high(c, h, q).wait_recv()
            value = value + high_in[c, q - 1, :, cols(h)].astype(jnp.float32)
        errors = value + bias_ref[:, cols(h)] - targets_ref[c, :, cols(h)].astype(jnp.float32)
        errors_ref[c, :, cols(h)] = errors
        gath[c, x, zl, zh, :, cols(h)] = errors.astype(jnp.bfloat16)
        for q in range(1, deep):
            give_z(c, h, q, mine).start()

    def pass_x(c, h):
        for q in range(1, deep):
            give_z(c, h, q, lax.rem(mine + deep - q, deep)).wait_recv()
        for q in range(1, m):
            give_x(c, h, q, x).start()

        @pl.when(layer > 0)
        def _():
            down(c, h, 0).start()

    def pass_down(c, h):
        for q in range(1, m):
            give_x(c, h, q, lax.rem(x + m - q, m)).wait_recv()

        @pl.when(layer > 0)
        def _():
            for q in range(1, m):
                down(c, h, q).start()

    def gradient(c, t):
        if t == 0:
            @pl.when(layer < layers - 1)
            def _():
                for h in range(PIECES):
                    for q in range(m):
                        down(c, h, q).wait_recv()

        grad = contract_width(gath[c].reshape(block, width), dec[0, feats(t), :])
        grad = grad + contract_width(foll[c].reshape(block, width), dec[1, feats(t), :])
        latent[:, feats(t)] = (grad * deriv[c, :, feats(t)].astype(jnp.float32)).astype(jnp.bfloat16)

    def weigh(c, t):
        value = lax.dot_general(
            acts[c].reshape(block, width), latent[:, feats(t)], (((0,), (0,)), ((), ())),
            preferred_element_type=jnp.float32,
        )
        if c > 0:
            value = total[:, feats(t)] + value
        if c < chunks - 1:
            total[:, feats(t)] = value
        else:
            enc[:, feats(t)] = (value * scale).astype(jnp.bfloat16)

    run = {
        "x": send_x, "low": send_low, "high": send_high, "give_z": send_errors,
        "give_x": pass_x, "down": pass_down, "gradient": gradient, "weigh": weigh,
    }
    inside, rest = plan(chunks, tiles)

    def every(c):
        return [load_acts(c, q, l) for q in range(m) for l in range(lo)]

    small = [
        pltpu.make_async_copy(source, place, small_sem.at[i])
        for i, (source, place) in enumerate(
            ((enc_bias_hbm, enc_bias_ref), (targets_hbm, targets_ref), (bias_hbm, bias_ref))
        )
    ]
    for copy in every(0):
        copy.start()
    small[0].start()
    for t in range(tiles):
        load_enc(t).start()

    @pl.when(layer == layers - 1)
    def _():
        foll[...] = jnp.zeros_like(foll)

    barrier = pltpu.get_barrier_semaphore()
    for to in (
        [(layer, at(zh, zl, x + q)) for q in range(1, m)]
        + [(layer, at(lax.rem(mine + q, hi), lax.rem(mine + q, deep) // hi, x)) for q in range(1, deep)]
        + [(above, me), (below, me)]
    ):
        pl.semaphore_signal(barrier, inc=1, device_id=to, device_id_type=MESH)

    for copy in every(0):
        copy.wait()
    small[0].wait()
    load_enc(0).wait()
    for i in range(slots):
        load_dec(i).start()
    for copy in small[1:]:
        copy.start()
    for c in range(1, chunks):
        for copy in every(c):
            copy.start()

    def split_dec(i):
        load_dec(i).wait()
        dec[:, pl.ds(pl.multiple_of(i * raws, raws), raws), :] = jnp.transpose(raw[lax.rem(i, slots)], (1, 0, 2))

        @pl.when(i + slots < parts)
        def _():
            load_dec(i + slots).start()

    encode(0, 0)
    pl.loop(0, slots)(split_dec)
    for t in range(1, tiles):
        load_enc(t).wait()
        encode(0, t)
    pl.loop(slots, parts)(split_dec)

    for copy in small[1:]:
        copy.wait()
    for c in range(1, chunks):
        for copy in every(c):
            copy.wait()

    pl.semaphore_wait(barrier, m + deep)

    @pl.loop(0, chunks)
    def _(c):
        def attend(spot):
            for back, stage, h in inside[spot]:
                @pl.when(c >= back)
                def _():
                    run[stage](c - back, h)

        decode_later(c, 0)
        attend(0)
        decode_later(c, 1)
        attend(1)
        decode_own(c, 0)
        attend(2)
        decode_own(c, 1)
        attend(3)

        @pl.when(c < chunks - 1)
        def _():
            for t in range(tiles):
                encode(c + 1, t)
                if t < 2:
                    attend(4 + t)

    for stage, c, k in rest:
        run[stage](c, k)

    @pl.loop(0, chunks)
    def _(c):
        for h in range(PIECES):
            for q in range(1, m):
                add_x(c, h, q).wait_send()
                give_x(c, h, q, x).wait_send()
            for q in range(1, lo):
                add_low(c, h, q).wait_send()
            for q in range(1, hi):
                add_high(c, h, q).wait_send()
            for q in range(1, deep):
                give_z(c, h, q, mine).wait_send()

            @pl.when(layer > 0)
            def _():
                for q in range(m):
                    down(c, h, q).wait_send()


def step(layers, tokens, acts, enc, dec, enc_bias, targets, bias):
    hi, lo, m, chunks, rows, width = acts.shape
    features = enc.shape[1]
    block = tokens // chunks
    half, full = jnp.bfloat16, jnp.float32
    vmem = pl.BlockSpec(memory_space=pltpu.VMEM)
    outside = pl.BlockSpec(memory_space=pltpu.HBM)
    dma = pltpu.SemaphoreType.DMA
    raws = 256
    parts = features // raws
    slots = -(-parts // 2)
    pairs = [(), (m - 1,), (lo - 1,), (hi - 1,), (lo * hi - 1,), (m - 1,), (m,)]
    return pl.pallas_call(
        functools.partial(step_kernel, layers, m, lo, hi, tokens ** (-0.5)),
        out_shape=(
            jax.ShapeDtypeStruct((chunks, rows, width), full),
            jax.ShapeDtypeStruct((width, features), half),
        ),
        in_specs=[outside] * 6,
        out_specs=(vmem, vmem),
        scratch_shapes=[
            pltpu.VMEM(enc_bias.shape, full),
            pltpu.VMEM(targets.shape, half),
            pltpu.VMEM(bias.shape, full),
            pltpu.VMEM((chunks, m, lo, hi, rows, width), half),
            pltpu.VMEM((slots, raws, 2, width), half),
            pltpu.VMEM((2, features, width), half),
            pltpu.VMEM((chunks, block, features), half),
            pltpu.VMEM((block, features), half),
            pltpu.VMEM((block, width), full),
            pltpu.VMEM((width, features), full),
            pltpu.VMEM((chunks, m, lo, hi, rows, width), half),
            pltpu.VMEM((chunks, m, lo, hi, rows, width), half),
            pltpu.VMEM((chunks, m, lo, hi, rows, width), half),
            pltpu.VMEM((chunks, m - 1, lo, hi, rows, width), half),
            pltpu.VMEM((chunks, lo - 1, hi, rows, width), half),
            pltpu.VMEM((chunks, hi - 1, rows, width), half),
            pltpu.VMEM((chunks, m, lo, hi, rows, width), half),
            pltpu.VMEM((chunks, m, lo, hi, rows, width), half),
            dma((3,)),
            dma((chunks, m, lo)),
            dma((features // tile_of(features),)),
            dma((parts,)),
            *[dma((chunks, PIECES, *p)) for p in pairs for _ in range(2)],
        ],
        compiler_params=pltpu.CompilerParams(
            collective_id=0, has_side_effects=True, vmem_limit_bytes=46 * 2**20
        ),
        name="step",
    )(*[pltpu.with_memory_space_constraint(a, pltpu.HBM) for a in (acts, enc, dec, enc_bias, targets, bias)])


def local(layers, n, acts, targets, enc_weight, enc_bias, dec_weight, dec_bias):
    tokens, width = acts.shape[1:]
    m = inner_of(n)
    lo = inner_of(n // m)
    rows = tokens // n
    chunks = chunks_of(rows)
    errors, enc_grad = step(
        layers, tokens,
        acts.reshape(n // (m * lo), lo, m, chunks, rows // chunks, width),
        enc_weight[0], dec_weight[0], enc_bias,
        targets.reshape(chunks, rows // chunks, width), dec_bias,
    )
    return (errors.reshape(1, rows, width), enc_grad[None])


def solution(mesh):
    return jax.shard_map(
        functools.partial(local, mesh.shape["layer"], mesh.shape["feat"]),
        mesh=mesh,
        in_specs=(
            P("layer", None, None),
            P("layer", "feat", None),
            P("layer", None, "feat"),
            P("layer", "feat"),
            P("layer", "feat", None, None),
            P("layer", None),
        ),
        out_specs=(P("layer", "feat", None), P("layer", None, "feat")),
        check_vma=False,
    )
```

```python
import functools
import math

import jax
import jax.numpy as jnp
from jax import lax
from jax.experimental import pallas as pl
from jax.experimental.pallas import tpu as pltpu
from jax.sharding import PartitionSpec as P

MESH = pl.DeviceIdType.MESH
PIECES = 4
DOTS = 2


def inner_of(n):
    return max(d for d in range(1, n + 1) if n % d == 0 and d * d <= n)


def chunks_of(rows):
    return next((c for c in (3, 2) if rows % (16 * c) == 0), 1)


def tile_of(features):
    return features // 2 if features % 256 == 0 else features


def contract_width(errs, decoder):
    return lax.dot_general(
        errs, decoder, (((1,), (1,)), ((), ())), preferred_element_type=jnp.float32
    )


SPOTS = {
    "x": (2, 4, 5, 6),
    "low": (5, 6, 9, 9),
    "high": (9, 10, 11, 12),
    "give_z": (11, 12, 14, 15),
    "give_x": (14, 29, 23, 26),
    "down": (32, 31, 33, 44),
}
REST = {
    "x": ((0, 0, 0, 0), (0, 0, 0, 0), (0, 1, 0, 3)),
    "low": ((0, 0, 0, 0), (0, 0, 0, 0), (10, 15, 9, 27)),
    "high": ((0, 0, 0, 0), (0, 2, 4, 8), (22, 25, 24, 34)),
    "give_z": ((0, 0, 0, 0), (5, 6, 21, 23), (35, 39, 42, 49)),
    "give_x": ((0, 16, 14, 19), (30, 26, 40, 38), (50, 53, 52, 56)),
    "down": ((31, 20, 18, 28), (41, 33, 47, 48), (57, 60, 59, 62)),
    "gradient": ((32, 44), (54, 58), (64, 65)),
    "weigh": ((45, 51), (61, 63), (66, 67)),
}


def plan(chunks, tiles):
    inside, rest = [[] for _ in range(6)], []
    ends = len(REST["x"])

    def rank(stage, c, k):
        rows = REST[stage]
        return (rows[max(0, min(c, ends - 1 - (chunks - 1 - c)))][k], c)

    for stage, spots in SPOTS.items():
        for h, place in enumerate(spots):
            back, spot = divmod(place, 6)
            inside[spot].append((back, stage, h))
            final = chunks - 1 if spot < 4 else chunks - 2
            rest += [(stage, c, h) for c in range(chunks) if c + back > final]
    for spot in inside:
        spot.sort(key=lambda e: -e[0])
    rest += [(stage, c, t) for c in range(chunks) for stage in ("gradient", "weigh") for t in range(tiles)]
    return inside, sorted(rest, key=lambda e: rank(*e))


def step_kernel(
    layers, m, lo, hi, scale, acts_hbm, enc_hbm, dec_hbm, enc_bias_hbm, targets_hbm, bias_hbm,
    errors_ref, enc,
    enc_bias_ref, targets_ref, bias_ref, acts, raw, dec, deriv, latent, own, total, later, arrived, sums, near, low_in, high_in, gath, foll,
    small_sem, acts_sem, enc_sem, dec_sem, up_send, up_recv, x_send, x_recv, low_send, low_recv, high_send, high_recv,
    gz_send, gz_recv, gx_send, gx_recv, down_send, down_recv,
):
    layer = lax.axis_index("layer")
    me = lax.axis_index("feat")
    x = lax.rem(me, m)
    zl, zh = lax.rem(me // m, lo), me // (m * lo)
    above = lax.rem(layer + 1, layers)
    below = lax.rem(layer + layers - 1, layers)
    chunks, rows, width = later.shape[0], *later.shape[4:]
    block = m * lo * hi * rows
    features = enc.shape[1]
    tile = tile_of(features)
    tiles = features // tile
    slots, raws = raw.shape[:2]
    parts = features // raws
    deep, mine = lo * hi, zl * hi + zh
    wide = width // PIECES
    dot = width // DOTS

    def at(h, l, xx):
        return (lax.rem(h, hi) * lo + lax.rem(l, lo)) * m + lax.rem(xx, m)

    def cols(h):
        return pl.ds(h * wide, wide)

    def dots(d):
        return pl.ds(d * dot, dot)

    def feats(t):
        return pl.ds(pl.multiple_of(t * tile, tile), tile)

    def remote(src, dst, send, recv, where):
        return pltpu.make_async_remote_copy(
            src_ref=src, dst_ref=dst, send_sem=send, recv_sem=recv,
            device_id=where, device_id_type=MESH,
        )

    def load_acts(c, q, l):
        return pltpu.make_async_copy(acts_hbm.at[:, l, q, c], acts.at[c, q, l], acts_sem.at[c, q, l])

    def load_enc(t):
        return pltpu.make_async_copy(enc_hbm.at[:, feats(t)], enc.at[:, feats(t)], enc_sem.at[t])

    def load_dec(i):
        part = pl.ds(pl.multiple_of(i * raws, raws), raws)
        return pltpu.make_async_copy(dec_hbm.at[part], raw.at[lax.rem(i, slots)], dec_sem.at[i])

    def up(c, h):
        return remote(
            later.at[c, :, :, :, :, cols(h)], arrived.at[c, :, :, :, :, cols(h)],
            up_send.at[c, h], up_recv.at[c, h], (above, me),
        )

    def add_x(c, h, q):
        to = lax.rem(x + q, m)
        return remote(
            sums.at[c, to, :, :, :, cols(h)], near.at[c, q - 1, :, :, :, cols(h)],
            x_send.at[c, h, q - 1], x_recv.at[c, h, q - 1], (layer, at(zh, zl, to)),
        )

    def add_low(c, h, q):
        to = lax.rem(zl + q, lo)
        return remote(
            later.at[c, 0, to, :, :, cols(h)], low_in.at[c, q - 1, :, :, cols(h)],
            low_send.at[c, h, q - 1], low_recv.at[c, h, q - 1], (layer, at(zh, to, x)),
        )

    def add_high(c, h, q):
        to = lax.rem(zh + q, hi)
        return remote(
            later.at[c, 0, zl, to, :, cols(h)], high_in.at[c, q - 1, :, cols(h)],
            high_send.at[c, h, q - 1], high_recv.at[c, h, q - 1], (layer, at(to, zl, x)),
        )

    def give_z(c, h, q, owner):
        spot = gath.at[c, x, owner // hi, lax.rem(owner, hi), :, cols(h)]
        to = lax.rem(mine + q, deep)
        return remote(
            spot, spot, gz_send.at[c, h, q - 1], gz_recv.at[c, h, q - 1], (layer, at(lax.rem(to, hi), to // hi, x))
        )

    def give_x(c, h, q, owner):
        spot = gath.at[c, owner, :, :, :, cols(h)]
        return remote(
            spot, spot, gx_send.at[c, h, q - 1], gx_recv.at[c, h, q - 1], (layer, at(zh, zl, x + q))
        )

    def down(c, h, q):
        owner = lax.rem(x + m - q, m)
        return remote(
            gath.at[c, owner, :, :, :, cols(h)], foll.at[c, owner, :, :, :, cols(h)],
            down_send.at[c, h, q], down_recv.at[c, h, q], (below, me),
        )

    def encode(c, t):
        lhs = acts[c].reshape(block, width)
        pre = jnp.dot(lhs, enc[:, feats(t)], preferred_element_type=jnp.float32)
        pre = pre + enc_bias_ref[:, feats(t)]
        shrunk = jnp.exp2(jnp.abs(pre) * (-4.0 * math.log2(math.e)))
        grown = 1.0 + shrunk
        part = 1.0 / grown
        lost = shrunk - (grown - 1.0)
        soft = jnp.log2(grown) * (0.25 * math.log(2.0)) + lost * (part * 0.25)
        latent[:, feats(t)] = (jnp.maximum(pre, 0.0) + soft).astype(jnp.bfloat16)
        deriv[c, :, feats(t)] = jnp.where(pre >= 0.0, part, shrunk * part).astype(jnp.bfloat16)

    def decode_later(c, d):
        value = jnp.dot(latent[...], dec[1, :, dots(d)], preferred_element_type=jnp.float32)
        later[c, :, :, :, :, dots(d)] = value.astype(jnp.bfloat16).reshape(m, lo, hi, rows, dot)

        @pl.when(layer < layers - 1)
        def _():
            for h in range(d * PIECES // DOTS, (d + 1) * PIECES // DOTS):
                up(c, h).start()

    def decode_own(c, d):
        own[:, dots(d)] = jnp.dot(
            latent[...], dec[0, :, dots(d)], preferred_element_type=jnp.float32
        )

    def send_x(c, h):
        @pl.when(layer > 0)
        def _():
            up(c, h).wait_recv()

        carried = jnp.where(layer > 0, arrived[c, :, :, :, :, cols(h)].reshape(block, wide).astype(jnp.float32), 0.0)
        both = (own[:, cols(h)] + carried).astype(jnp.bfloat16)
        sums[c, :, :, :, :, cols(h)] = both.reshape(m, lo, hi, rows, wide)
        for q in range(1, m):
            add_x(c, h, q).start()

    def send_low(c, h):
        value = sums[c, x, :, :, :, cols(h)].astype(jnp.float32)
        for q in range(1, m):
            add_x(c, h, q).wait_recv()
            value = value + near[c, q - 1, :, :, :, cols(h)].astype(jnp.float32)

        @pl.when(layer < layers - 1)
        def _():
            up(c, h).wait_send()

        later[c, 0, :, :, :, cols(h)] = value.astype(jnp.bfloat16)
        for q in range(1, lo):
            add_low(c, h, q).start()

    def own_low(c, h, spot):
        value = sums[c, x, zl, spot, :, cols(h)].astype(jnp.float32)
        for q in range(1, m):
            value = value + near[c, q - 1, zl, spot, :, cols(h)].astype(jnp.float32)
        for q in range(1, lo):
            value = value + low_in[c, q - 1, spot, :, cols(h)].astype(jnp.float32)
        return value

    def send_high(c, h):
        for q in range(1, lo):
            add_low(c, h, q).wait_recv()
        for q in range(1, hi):
            to = lax.rem(zh + q, hi)
            later[c, 0, zl, to, :, cols(h)] = own_low(c, h, to).astype(jnp.bfloat16)
            add_high(c, h, q).start()

    def send_errors(c, h):
        value = own_low(c, h, zh)
        for q in range(1, hi):
            add_high(c, h, q).wait_recv()
            value = value + high_in[c, q - 1, :, cols(h)].astype(jnp.float32)
        errors = value + bias_ref[:, cols(h)] - targets_ref[c, :, cols(h)].astype(jnp.float32)
        errors_ref[c, :, cols(h)] = errors
        gath[c, x, zl, zh, :, cols(h)] = errors.astype(jnp.bfloat16)
        for q in range(1, deep):
            give_z(c, h, q, mine).start()

    def pass_x(c, h):
        for q in range(1, deep):
            give_z(c, h, q, lax.rem(mine + deep - q, deep)).wait_recv()
        for q in range(1, m):
            give_x(c, h, q, x).start()

        @pl.when(layer > 0)
        def _():
            down(c, h, 0).start()

    def pass_down(c, h):
        for q in range(1, m):
            give_x(c, h, q, lax.rem(x + m - q, m)).wait_recv()

        @pl.when(layer > 0)
        def _():
            for q in range(1, m):
                down(c, h, q).start()

    def gradient(c, t):
        if t == 0:
            @pl.when(layer < layers - 1)
            def _():
                for h in range(PIECES):
                    for q in range(m):
                        down(c, h, q).wait_recv()

        grad = contract_width(gath[c].reshape(block, width), dec[0, feats(t), :])
        grad = grad + contract_width(foll[c].reshape(block, width), dec[1, feats(t), :])
        latent[:, feats(t)] = (grad * deriv[c, :, feats(t)].astype(jnp.float32)).astype(jnp.bfloat16)

    def weigh(c, t):
        value = lax.dot_general(
            acts[c].reshape(block, width), latent[:, feats(t)], (((0,), (0,)), ((), ())),
            preferred_element_type=jnp.float32,
        )
        if c > 0:
            value = total[:, feats(t)] + value
        if c < chunks - 1:
            total[:, feats(t)] = value
        else:
            enc[:, feats(t)] = (value * scale).astype(jnp.bfloat16)

    run = {
        "x": send_x, "low": send_low, "high": send_high, "give_z": send_errors,
        "give_x": pass_x, "down": pass_down, "gradient": gradient, "weigh": weigh,
    }
    inside, rest = plan(chunks, tiles)

    def every(c):
        return [load_acts(c, q, l) for q in range(m) for l in range(lo)]

    small = [
        pltpu.make_async_copy(source, place, small_sem.at[i])
        for i, (source, place) in enumerate(
            ((enc_bias_hbm, enc_bias_ref), (targets_hbm, targets_ref), (bias_hbm, bias_ref))
        )
    ]
    for copy in every(0):
        copy.start()
    small[0].start()
    for t in range(tiles):
        load_enc(t).start()

    @pl.when(layer == layers - 1)
    def _():
        foll[...] = jnp.zeros_like(foll)

    barrier = pltpu.get_barrier_semaphore()
    for to in (
        [(layer, at(zh, zl, x + q)) for q in range(1, m)]
        + [(layer, at(lax.rem(mine + q, hi), lax.rem(mine + q, deep) // hi, x)) for q in range(1, deep)]
        + [(above, me), (below, me)]
    ):
        pl.semaphore_signal(barrier, inc=1, device_id=to, device_id_type=MESH)

    for copy in every(0):
        copy.wait()
    small[0].wait()
    load_enc(0).wait()
    for i in range(slots):
        load_dec(i).start()
    for copy in small[1:]:
        copy.start()
    for c in range(1, chunks):
        for copy in every(c):
            copy.start()

    def split_dec(i):
        load_dec(i).wait()
        dec[:, pl.ds(pl.multiple_of(i * raws, raws), raws), :] = jnp.transpose(raw[lax.rem(i, slots)], (1, 0, 2))

        @pl.when(i + slots < parts)
        def _():
            load_dec(i + slots).start()

    encode(0, 0)
    pl.loop(0, slots)(split_dec)
    for t in range(1, tiles):
        load_enc(t).wait()
        encode(0, t)
    pl.loop(slots, parts)(split_dec)

    for copy in small[1:]:
        copy.wait()
    for c in range(1, chunks):
        for copy in every(c):
            copy.wait()

    pl.semaphore_wait(barrier, m + deep)

    @pl.loop(0, chunks)
    def _(c):
        def attend(spot):
            for back, stage, h in inside[spot]:
                @pl.when(c >= back)
                def _():
                    run[stage](c - back, h)

        decode_later(c, 0)
        attend(0)
        decode_later(c, 1)
        attend(1)
        decode_own(c, 0)
        attend(2)
        decode_own(c, 1)
        attend(3)

        @pl.when(c < chunks - 1)
        def _():
            for t in range(tiles):
                encode(c + 1, t)
                if t < 2:
                    attend(4 + t)

    for stage, c, k in rest:
        run[stage](c, k)

    @pl.loop(0, chunks)
    def _(c):
        for h in range(PIECES):
            for q in range(1, m):
                add_x(c, h, q).wait_send()
                give_x(c, h, q, x).wait_send()
            for q in range(1, lo):
                add_low(c, h, q).wait_send()
            for q in range(1, hi):
                add_high(c, h, q).wait_send()
            for q in range(1, deep):
                give_z(c, h, q, mine).wait_send()

            @pl.when(layer > 0)
            def _():
                for q in range(m):
                    down(c, h, q).wait_send()


def step(layers, tokens, acts, enc, dec, enc_bias, targets, bias):
    hi, lo, m, chunks, rows, width = acts.shape
    features = enc.shape[1]
    block = tokens // chunks
    half, full = jnp.bfloat16, jnp.float32
    vmem = pl.BlockSpec(memory_space=pltpu.VMEM)
    outside = pl.BlockSpec(memory_space=pltpu.HBM)
    dma = pltpu.SemaphoreType.DMA
    raws = 256
    parts = features // raws
    slots = -(-parts // 2)
    pairs = [(), (m - 1,), (lo - 1,), (hi - 1,), (lo * hi - 1,), (m - 1,), (m,)]
    return pl.pallas_call(
        functools.partial(step_kernel, layers, m, lo, hi, tokens ** (-0.5)),
        out_shape=(
            jax.ShapeDtypeStruct((chunks, rows, width), full),
            jax.ShapeDtypeStruct((width, features), half),
        ),
        in_specs=[outside] * 6,
        out_specs=(vmem, vmem),
        scratch_shapes=[
            pltpu.VMEM(enc_bias.shape, full),
            pltpu.VMEM(targets.shape, half),
            pltpu.VMEM(bias.shape, full),
            pltpu.VMEM((chunks, m, lo, hi, rows, width), half),
            pltpu.VMEM((slots, raws, 2, width), half),
            pltpu.VMEM((2, features, width), half),
            pltpu.VMEM((chunks, block, features), half),
            pltpu.VMEM((block, features), half),
            pltpu.VMEM((block, width), full),
            pltpu.VMEM((width, features), full),
            pltpu.VMEM((chunks, m, lo, hi, rows, width), half),
            pltpu.VMEM((chunks, m, lo, hi, rows, width), half),
            pltpu.VMEM((chunks, m, lo, hi, rows, width), half),
            pltpu.VMEM((chunks, m - 1, lo, hi, rows, width), half),
            pltpu.VMEM((chunks, lo - 1, hi, rows, width), half),
            pltpu.VMEM((chunks, hi - 1, rows, width), half),
            pltpu.VMEM((chunks, m, lo, hi, rows, width), half),
            pltpu.VMEM((chunks, m, lo, hi, rows, width), half),
            dma((3,)),
            dma((chunks, m, lo)),
            dma((features // tile_of(features),)),
            dma((parts,)),
            *[dma((chunks, PIECES, *p)) for p in pairs for _ in range(2)],
        ],
        compiler_params=pltpu.CompilerParams(
            collective_id=0, has_side_effects=True, vmem_limit_bytes=46 * 2**20
        ),
        name="step",
    )(*[pltpu.with_memory_space_constraint(a, pltpu.HBM) for a in (acts, enc, dec, enc_bias, targets, bias)])


def local(layers, n, acts, targets, enc_weight, enc_bias, dec_weight, dec_bias):
    tokens, width = acts.shape[1:]
    m = inner_of(n)
    lo = inner_of(n // m)
    rows = tokens // n
    chunks = chunks_of(rows)
    errors, enc_grad = step(
        layers, tokens,
        acts.reshape(n // (m * lo), lo, m, chunks, rows // chunks, width),
        enc_weight[0], dec_weight[0], enc_bias,
        targets.reshape(chunks, rows // chunks, width), dec_bias,
    )
    return (errors.reshape(1, rows, width), enc_grad[None])


def solution(mesh):
    return jax.shard_map(
        functools.partial(local, mesh.shape["layer"], mesh.shape["feat"]),
        mesh=mesh,
        in_specs=(
            P("layer", None, None),
            P("layer", "feat", None),
            P("layer", None, "feat"),
            P("layer", "feat"),
            P("layer", "feat", None, None),
            P("layer", None),
        ),
        out_specs=(P("layer", "feat", None), P("layer", None, "feat")),
        check_vma=False,
    )
```

```python
import functools
import math

import jax
import jax.numpy as jnp
from jax import lax
from jax.experimental import pallas as pl
from jax.experimental.pallas import tpu as pltpu
from jax.sharding import PartitionSpec as P

MESH = pl.DeviceIdType.MESH
PIECES = 4
DOTS = 2


def inner_of(n):
    return max(d for d in range(1, n + 1) if n % d == 0 and d * d <= n)


def chunks_of(rows):
    return next((c for c in (3, 2) if rows % (16 * c) == 0), 1)


def tile_of(features):
    return features // 2 if features % 256 == 0 else features


def contract_width(errs, decoder):
    return lax.dot_general(
        errs, decoder, (((1,), (1,)), ((), ())), preferred_element_type=jnp.float32
    )


SPOTS = {
    "x": (3, 4, 6, 6),
    "low": (5, 7, 9, 9),
    "high": (8, 10, 12, 12),
    "give_z": (10, 13, 17, 15),
    "give_x": (14, 16, 20, 19),
    "down": (47, 29, 23, 26),
}
REST = {
    "x": ((0, 0, 0, 0), (0, 0, 0, 0), (0, 0, 2, 1)),
    "low": ((0, 0, 0, 0), (0, 0, 0, 0), (8, 10, 16, 13)),
    "high": ((0, 0, 0, 0), (0, 5, 9, 14), (19, 22, 31, 28)),
    "give_z": ((0, 0, 3, 0), (7, 11, 20, 26), (32, 37, 46, 44)),
    "give_x": ((0, 6, 12, 21), (18, 30, 39, 41), (51, 53, 55, 54)),
    "down": ((25, 15, 23, 29), (27, 43, 49, 48), (58, 59, 61, 62)),
    "contribute": ((33, 0), (56, 0), (65, 0)),
    "gradient": ((34, 42), (57, 60), (66, 67)),
    "weigh": ((47, 52), (63, 64), (68, 69)),
}


def plan(chunks, tiles):
    inside, rest = [[] for _ in range(6)], []
    ends = len(REST["x"])

    def rank(stage, c, k):
        rows = REST[stage]
        return (rows[max(0, min(c, ends - 1 - (chunks - 1 - c)))][k], c)

    for stage, spots in SPOTS.items():
        for h, place in enumerate(spots):
            back, spot = divmod(place, 6)
            inside[spot].append((back, stage, h))
            final = chunks - 1 if spot < 4 else chunks - 2
            rest += [(stage, c, h) for c in range(chunks) if c + back > final]
    for spot in inside:
        spot.sort(key=lambda e: -e[0])
    rest += [("contribute", c, 0) for c in range(chunks)]
    rest += [(stage, c, t) for c in range(chunks) for stage in ("gradient", "weigh") for t in range(tiles)]
    return inside, sorted(rest, key=lambda e: rank(*e))


def step_kernel(
    layers, m, lo, hi, scale, acts_hbm, enc_hbm, dec_hbm, enc_bias_hbm, targets_hbm, bias_hbm,
    errors_ref, enc,
    enc_bias_ref, targets_ref, bias_ref, acts, raw, dec, deriv, latent, own, total, later, arrived, sums, near, low_in, high_in, gath, foll,
    small_sem, acts_sem, enc_sem, dec_sem, up_send, up_recv, x_send, x_recv, low_send, low_recv, high_send, high_recv,
    gz_send, gz_recv, gx_send, gx_recv, down_send, down_recv,
):
    layer = lax.axis_index("layer")
    me = lax.axis_index("feat")
    x = lax.rem(me, m)
    zl, zh = lax.rem(me // m, lo), me // (m * lo)
    above = lax.rem(layer + 1, layers)
    below = lax.rem(layer + layers - 1, layers)
    chunks, rows, width = later.shape[0], *later.shape[4:]
    block = m * lo * hi * rows
    features = enc.shape[1]
    tile = tile_of(features)
    tiles = features // tile
    slots, raws = raw.shape[:2]
    parts = features // raws
    deep, mine = lo * hi, zl * hi + zh
    wide = width // PIECES
    dot = width // DOTS

    def at(h, l, xx):
        return (lax.rem(h, hi) * lo + lax.rem(l, lo)) * m + lax.rem(xx, m)

    def cols(h):
        return pl.ds(h * wide, wide)

    def dots(d):
        return pl.ds(d * dot, dot)

    def feats(t):
        return pl.ds(pl.multiple_of(t * tile, tile), tile)

    def remote(src, dst, send, recv, where):
        return pltpu.make_async_remote_copy(
            src_ref=src, dst_ref=dst, send_sem=send, recv_sem=recv,
            device_id=where, device_id_type=MESH,
        )

    def load_acts(c, q, l):
        return pltpu.make_async_copy(acts_hbm.at[:, l, q, c], acts.at[c, q, l], acts_sem.at[c, q, l])

    def load_enc(t):
        return pltpu.make_async_copy(enc_hbm.at[:, feats(t)], enc.at[:, feats(t)], enc_sem.at[t])

    def load_dec(i):
        part = pl.ds(pl.multiple_of(i * raws, raws), raws)
        return pltpu.make_async_copy(dec_hbm.at[part], raw.at[lax.rem(i, slots)], dec_sem.at[i])

    def up(c, h):
        return remote(
            later.at[c, :, :, :, :, cols(h)], arrived.at[c, :, :, :, :, cols(h)],
            up_send.at[c, h], up_recv.at[c, h], (above, me),
        )

    def add_x(c, h, q):
        to = lax.rem(x + q, m)
        return remote(
            sums.at[c, to, :, :, :, cols(h)], near.at[c, q - 1, :, :, :, cols(h)],
            x_send.at[c, h, q - 1], x_recv.at[c, h, q - 1], (layer, at(zh, zl, to)),
        )

    def add_low(c, h, q):
        to = lax.rem(zl + q, lo)
        return remote(
            later.at[c, 0, to, :, :, cols(h)], low_in.at[c, q - 1, :, :, cols(h)],
            low_send.at[c, h, q - 1], low_recv.at[c, h, q - 1], (layer, at(zh, to, x)),
        )

    def add_high(c, h, q):
        to = lax.rem(zh + q, hi)
        return remote(
            later.at[c, 0, zl, to, :, cols(h)], high_in.at[c, q - 1, :, cols(h)],
            high_send.at[c, h, q - 1], high_recv.at[c, h, q - 1], (layer, at(to, zl, x)),
        )

    def give_z(c, h, q, owner):
        spot = gath.at[c, x, owner // hi, lax.rem(owner, hi), :, cols(h)]
        to = lax.rem(mine + q, deep)
        return remote(
            spot, spot, gz_send.at[c, h, q - 1], gz_recv.at[c, h, q - 1], (layer, at(lax.rem(to, hi), to // hi, x))
        )

    def give_x(c, h, q, owner):
        spot = gath.at[c, owner, :, :, :, cols(h)]
        return remote(
            spot, spot, gx_send.at[c, h, q - 1], gx_recv.at[c, h, q - 1], (layer, at(zh, zl, x + q))
        )

    def down(c, h, q):
        owner = lax.rem(x + m - q, m)
        return remote(
            gath.at[c, owner, :, :, :, cols(h)], foll.at[c, owner, :, :, :, cols(h)],
            down_send.at[c, h, q], down_recv.at[c, h, q], (below, me),
        )

    def encode(c, t):
        lhs = acts[c].reshape(block, width)
        pre = jnp.dot(lhs, enc[:, feats(t)], preferred_element_type=jnp.float32)
        pre = pre + enc_bias_ref[:, feats(t)]
        shrunk = jnp.exp2(jnp.abs(pre) * (-4.0 * math.log2(math.e)))
        grown = 1.0 + shrunk
        part = 1.0 / grown
        lost = shrunk - (grown - 1.0)
        soft = jnp.log2(grown) * (0.25 * math.log(2.0)) + lost * (part * 0.25)
        latent[:, feats(t)] = (jnp.maximum(pre, 0.0) + soft).astype(jnp.bfloat16)
        deriv[c, :, feats(t)] = jnp.where(pre >= 0.0, part, shrunk * part).astype(jnp.bfloat16)

    def decode_later(c, d):
        value = jnp.dot(latent[...], dec[1, :, dots(d)], preferred_element_type=jnp.float32)
        later[c, :, :, :, :, dots(d)] = value.astype(jnp.bfloat16).reshape(m, lo, hi, rows, dot)

        @pl.when(layer < layers - 1)
        def _():
            for h in range(d * PIECES // DOTS, (d + 1) * PIECES // DOTS):
                up(c, h).start()

    def decode_own(c, d):
        own[:, dots(d)] = jnp.dot(
            latent[...], dec[0, :, dots(d)], preferred_element_type=jnp.float32
        )

    def send_x(c, h):
        @pl.when(layer > 0)
        def _():
            up(c, h).wait_recv()

        carried = jnp.where(layer > 0, arrived[c, :, :, :, :, cols(h)].reshape(block, wide).astype(jnp.float32), 0.0)
        both = (own[:, cols(h)] + carried).astype(jnp.bfloat16)
        sums[c, :, :, :, :, cols(h)] = both.reshape(m, lo, hi, rows, wide)
        for q in range(1, m):
            add_x(c, h, q).start()

    def send_low(c, h):
        value = sums[c, x, :, :, :, cols(h)].astype(jnp.float32)
        for q in range(1, m):
            add_x(c, h, q).wait_recv()
            value = value + near[c, q - 1, :, :, :, cols(h)].astype(jnp.float32)

        @pl.when(layer < layers - 1)
        def _():
            up(c, h).wait_send()

        later[c, 0, :, :, :, cols(h)] = value.astype(jnp.bfloat16)
        for q in range(1, lo):
            add_low(c, h, q).start()

    def own_low(c, h, spot):
        value = sums[c, x, zl, spot, :, cols(h)].astype(jnp.float32)
        for q in range(1, m):
            value = value + near[c, q - 1, zl, spot, :, cols(h)].astype(jnp.float32)
        for q in range(1, lo):
            value = value + low_in[c, q - 1, spot, :, cols(h)].astype(jnp.float32)
        return value

    def send_high(c, h):
        for q in range(1, lo):
            add_low(c, h, q).wait_recv()
        for q in range(1, hi):
            to = lax.rem(zh + q, hi)
            later[c, 0, zl, to, :, cols(h)] = own_low(c, h, to).astype(jnp.bfloat16)
            add_high(c, h, q).start()

    def send_errors(c, h):
        value = own_low(c, h, zh)
        for q in range(1, hi):
            add_high(c, h, q).wait_recv()
            value = value + high_in[c, q - 1, :, cols(h)].astype(jnp.float32)
        errors = value + bias_ref[:, cols(h)] - targets_ref[c, :, cols(h)].astype(jnp.float32)
        errors_ref[c, :, cols(h)] = errors
        gath[c, x, zl, zh, :, cols(h)] = errors.astype(jnp.bfloat16)
        for q in range(1, deep):
            give_z(c, h, q, mine).start()

    def pass_x(c, h):
        for q in range(1, deep):
            give_z(c, h, q, lax.rem(mine + deep - q, deep)).wait_recv()
        for q in range(1, m):
            give_x(c, h, q, x).start()

        @pl.when(layer > 0)
        def _():
            down(c, h, 0).start()

    def pass_down(c, h):
        for q in range(1, m):
            give_x(c, h, q, lax.rem(x + m - q, m)).wait_recv()

        @pl.when(layer > 0)
        def _():
            for q in range(1, m):
                down(c, h, q).start()

    def contribute(c, t):
        own[:, :tile] = contract_width(gath[c].reshape(block, width), dec[0, feats(t), :])

    def gradient(c, t):
        if t == 0:
            @pl.when(layer < layers - 1)
            def _():
                for h in range(PIECES):
                    for q in range(m):
                        down(c, h, q).wait_recv()

            grad = own[:, :tile]
        else:
            grad = contract_width(gath[c].reshape(block, width), dec[0, feats(t), :])
        grad = grad + contract_width(foll[c].reshape(block, width), dec[1, feats(t), :])
        latent[:, feats(t)] = (grad * deriv[c, :, feats(t)].astype(jnp.float32)).astype(jnp.bfloat16)

    def weigh(c, t):
        value = lax.dot_general(
            acts[c].reshape(block, width), latent[:, feats(t)], (((0,), (0,)), ((), ())),
            preferred_element_type=jnp.float32,
        )
        if c > 0:
            value = total[:, feats(t)] + value
        if c < chunks - 1:
            total[:, feats(t)] = value
        else:
            enc[:, feats(t)] = (value * scale).astype(jnp.bfloat16)

    run = {
        "x": send_x, "low": send_low, "high": send_high, "give_z": send_errors,
        "give_x": pass_x, "down": pass_down, "contribute": contribute, "gradient": gradient, "weigh": weigh,
    }
    inside, rest = plan(chunks, tiles)

    def every(c):
        return [load_acts(c, q, l) for q in range(m) for l in range(lo)]

    small = [
        pltpu.make_async_copy(source, place, small_sem.at[i])
        for i, (source, place) in enumerate(
            ((enc_bias_hbm, enc_bias_ref), (targets_hbm, targets_ref), (bias_hbm, bias_ref))
        )
    ]
    for copy in every(0):
        copy.start()
    small[0].start()
    load_enc(0).start()

    @pl.when(layer == layers - 1)
    def _():
        foll[...] = jnp.zeros_like(foll)

    barrier = pltpu.get_barrier_semaphore()
    for to in (
        [(layer, at(zh, zl, x + q)) for q in range(1, m)]
        + [(layer, at(lax.rem(mine + q, hi), lax.rem(mine + q, deep) // hi, x)) for q in range(1, deep)]
        + [(above, me), (below, me)]
    ):
        pl.semaphore_signal(barrier, inc=1, device_id=to, device_id_type=MESH)

    for copy in every(0):
        copy.wait()
    small[0].wait()
    load_enc(0).wait()
    for i in range(slots):
        load_dec(i).start()
    for t in range(1, tiles):
        load_enc(t).start()
    for copy in small[1:]:
        copy.start()
    for c in range(1, chunks):
        for copy in every(c):
            copy.start()

    def split_dec(i):
        load_dec(i).wait()
        dec[:, pl.ds(pl.multiple_of(i * raws, raws), raws), :] = jnp.transpose(raw[lax.rem(i, slots)], (1, 0, 2))

        @pl.when(i + slots < parts)
        def _():
            load_dec(i + slots).start()

    encode(0, 0)
    pl.loop(0, slots)(split_dec)
    for t in range(1, tiles):
        load_enc(t).wait()
        encode(0, t)
    pl.loop(slots, parts)(split_dec)

    for copy in small[1:]:
        copy.wait()
    for c in range(1, chunks):
        for copy in every(c):
            copy.wait()

    pl.semaphore_wait(barrier, m + deep)

    @pl.loop(0, chunks)
    def _(c):
        def attend(spot):
            for back, stage, h in inside[spot]:
                @pl.when(c >= back)
                def _():
                    run[stage](c - back, h)

        decode_later(c, 0)
        attend(0)
        decode_later(c, 1)
        attend(1)
        decode_own(c, 0)
        attend(2)
        decode_own(c, 1)
        attend(3)

        @pl.when(c < chunks - 1)
        def _():
            for t in range(tiles):
                encode(c + 1, t)
                if t < 2:
                    attend(4 + t)

    for stage, c, k in rest:
        run[stage](c, k)

    @pl.loop(0, chunks)
    def _(c):
        for h in range(PIECES):
            for q in range(1, m):
                add_x(c, h, q).wait_send()
                give_x(c, h, q, x).wait_send()
            for q in range(1, lo):
                add_low(c, h, q).wait_send()
            for q in range(1, hi):
                add_high(c, h, q).wait_send()
            for q in range(1, deep):
                give_z(c, h, q, mine).wait_send()

            @pl.when(layer > 0)
            def _():
                for q in range(m):
                    down(c, h, q).wait_send()


def step(layers, tokens, acts, enc, dec, enc_bias, targets, bias):
    hi, lo, m, chunks, rows, width = acts.shape
    features = enc.shape[1]
    block = tokens // chunks
    half, full = jnp.bfloat16, jnp.float32
    vmem = pl.BlockSpec(memory_space=pltpu.VMEM)
    outside = pl.BlockSpec(memory_space=pltpu.HBM)
    dma = pltpu.SemaphoreType.DMA
    raws = 256
    parts = features // raws
    slots = -(-parts // 2)
    pairs = [(), (m - 1,), (lo - 1,), (hi - 1,), (lo * hi - 1,), (m - 1,), (m,)]
    return pl.pallas_call(
        functools.partial(step_kernel, layers, m, lo, hi, tokens ** (-0.5)),
        out_shape=(
            jax.ShapeDtypeStruct((chunks, rows, width), full),
            jax.ShapeDtypeStruct((width, features), half),
        ),
        in_specs=[outside] * 6,
        out_specs=(vmem, vmem),
        scratch_shapes=[
            pltpu.VMEM(enc_bias.shape, full),
            pltpu.VMEM(targets.shape, half),
            pltpu.VMEM(bias.shape, full),
            pltpu.VMEM((chunks, m, lo, hi, rows, width), half),
            pltpu.VMEM((slots, raws, 2, width), half),
            pltpu.VMEM((2, features, width), half),
            pltpu.VMEM((chunks, block, features), half),
            pltpu.VMEM((block, features), half),
            pltpu.VMEM((block, max(width, tile_of(features))), full),
            pltpu.VMEM((width, features), full),
            pltpu.VMEM((chunks, m, lo, hi, rows, width), half),
            pltpu.VMEM((chunks, m, lo, hi, rows, width), half),
            pltpu.VMEM((chunks, m, lo, hi, rows, width), half),
            pltpu.VMEM((chunks, m - 1, lo, hi, rows, width), half),
            pltpu.VMEM((chunks, lo - 1, hi, rows, width), half),
            pltpu.VMEM((chunks, hi - 1, rows, width), half),
            pltpu.VMEM((chunks, m, lo, hi, rows, width), half),
            pltpu.VMEM((chunks, m, lo, hi, rows, width), half),
            dma((3,)),
            dma((chunks, m, lo)),
            dma((features // tile_of(features),)),
            dma((parts,)),
            *[dma((chunks, PIECES, *p)) for p in pairs for _ in range(2)],
        ],
        compiler_params=pltpu.CompilerParams(
            collective_id=0, has_side_effects=True, vmem_limit_bytes=46 * 2**20
        ),
        name="step",
    )(*[pltpu.with_memory_space_constraint(a, pltpu.HBM) for a in (acts, enc, dec, enc_bias, targets, bias)])


def local(layers, n, acts, targets, enc_weight, enc_bias, dec_weight, dec_bias):
    tokens, width = acts.shape[1:]
    m = inner_of(n)
    lo = inner_of(n // m)
    rows = tokens // n
    chunks = chunks_of(rows)
    errors, enc_grad = step(
        layers, tokens,
        acts.reshape(n // (m * lo), lo, m, chunks, rows // chunks, width),
        enc_weight[0], dec_weight[0], enc_bias,
        targets.reshape(chunks, rows // chunks, width), dec_bias,
    )
    return (errors.reshape(1, rows, width), enc_grad[None])


def solution(mesh):
    return jax.shard_map(
        functools.partial(local, mesh.shape["layer"], mesh.shape["feat"]),
        mesh=mesh,
        in_specs=(
            P("layer", None, None),
            P("layer", "feat", None),
            P("layer", None, "feat"),
            P("layer", "feat"),
            P("layer", "feat", None, None),
            P("layer", None),
        ),
        out_specs=(P("layer", "feat", None), P("layer", None, "feat")),
        check_vma=False,
    )
```

```python
import functools
import math

import jax
import jax.numpy as jnp
from jax import lax
from jax.experimental import pallas as pl
from jax.experimental.pallas import tpu as pltpu
from jax.sharding import PartitionSpec as P

MESH = pl.DeviceIdType.MESH
PIECES = 4
DOTS = 2


def inner_of(n):
    return max(d for d in range(1, n + 1) if n % d == 0 and d * d <= n)


def chunks_of(rows):
    return next((c for c in (3, 2) if rows % (16 * c) == 0), 1)


def tile_of(features):
    return features // 2 if features % 256 == 0 else features


def contract_width(errs, decoder):
    return lax.dot_general(
        errs, decoder, (((1,), (1,)), ((), ())), preferred_element_type=jnp.float32
    )


SPOTS = {
    "x": (2, 4, 5, 7),
    "low": (6, 7, 8, 10),
    "high": (9, 10, 12, 14),
    "give_z": (11, 13, 22, 18),
    "give_x": (19, 26, 35, 29),
    "down": (48, 31, 65, 54),
}
REST = {
    "x": ((0, 0, 0, 0), (0, 0, 0, 0), (0, 2, 1, 5)),
    "low": ((0, 0, 0, 0), (0, 0, 0, 0), (12, 13, 18, 21)),
    "high": ((0, 0, 0, 0), (0, 3, 11, 14), (22, 26, 30, 42)),
    "give_z": ((0, 0, 7, 9), (16, 20, 23, 28), (39, 41, 44, 53)),
    "give_x": ((4, 6, 15, 19), (35, 33, 38, 45), (52, 55, 58, 62)),
    "down": ((17, 27, 29, 31), (43, 47, 50, 54), (60, 64, 65, 66)),
    "contribute": ((32, 0), (56, 0), (67, 0)),
    "gradient": ((36, 40), (59, 63), (70, 71)),
    "weigh": ((46, 48), (68, 69), (72, 73)),
}


def plan(chunks, tiles):
    inside, rest = [[] for _ in range(6)], []
    ends = len(REST["x"])

    def rank(stage, c, k):
        rows = REST[stage]
        return (rows[max(0, min(c, ends - 1 - (chunks - 1 - c)))][k], c)

    for stage, spots in SPOTS.items():
        for h, place in enumerate(spots):
            back, spot = divmod(place, 6)
            inside[spot].append((back, stage, h))
            final = chunks - 1 if spot < 4 else chunks - 2
            rest += [(stage, c, h) for c in range(chunks) if c + back > final]
    for spot in inside:
        spot.sort(key=lambda e: -e[0])
    rest += [("contribute", c, 0) for c in range(chunks)]
    rest += [(stage, c, t) for c in range(chunks) for stage in ("gradient", "weigh") for t in range(tiles)]
    return inside, sorted(rest, key=lambda e: rank(*e))


def step_kernel(
    layers, m, lo, hi, scale, acts_hbm, enc_hbm, dec_hbm, enc_bias_hbm, targets_hbm, bias_hbm,
    errors_ref, enc,
    enc_bias_ref, targets_ref, bias_ref, acts, raw, dec, deriv, latent, own, total, later, arrived, sums, near, low_in, high_in, gath, foll,
    small_sem, acts_sem, enc_sem, dec_sem, up_send, up_recv, x_send, x_recv, low_send, low_recv, high_send, high_recv,
    gz_send, gz_recv, gx_send, gx_recv, down_send, down_recv,
):
    layer = lax.axis_index("layer")
    me = lax.axis_index("feat")
    x = lax.rem(me, m)
    zl, zh = lax.rem(me // m, lo), me // (m * lo)
    above = lax.rem(layer + 1, layers)
    below = lax.rem(layer + layers - 1, layers)
    chunks, rows, width = later.shape[0], *later.shape[4:]
    block = m * lo * hi * rows
    features = enc.shape[1]
    tile = tile_of(features)
    tiles = features // tile
    slots, raws = raw.shape[:2]
    parts = features // raws
    deep, mine = lo * hi, zl * hi + zh
    wide = width // PIECES
    dot = width // DOTS

    def at(h, l, xx):
        return (lax.rem(h, hi) * lo + lax.rem(l, lo)) * m + lax.rem(xx, m)

    def cols(h):
        return pl.ds(h * wide, wide)

    def dots(d):
        return pl.ds(d * dot, dot)

    def feats(t):
        return pl.ds(pl.multiple_of(t * tile, tile), tile)

    def remote(src, dst, send, recv, where):
        return pltpu.make_async_remote_copy(
            src_ref=src, dst_ref=dst, send_sem=send, recv_sem=recv,
            device_id=where, device_id_type=MESH,
        )

    def load_acts(c, q, l):
        return pltpu.make_async_copy(acts_hbm.at[:, l, q, c], acts.at[c, q, l], acts_sem.at[c, q, l])

    def load_enc(t):
        return pltpu.make_async_copy(enc_hbm.at[:, feats(t)], enc.at[:, feats(t)], enc_sem.at[t])

    def load_dec(i):
        part = pl.ds(pl.multiple_of(i * raws, raws), raws)
        return pltpu.make_async_copy(dec_hbm.at[part], raw.at[lax.rem(i, slots)], dec_sem.at[i])

    def up(c, h):
        return remote(
            later.at[c, :, :, :, :, cols(h)], arrived.at[c, :, :, :, :, cols(h)],
            up_send.at[c, h], up_recv.at[c, h], (above, me),
        )

    def add_x(c, h, q):
        to = lax.rem(x + q, m)
        return remote(
            sums.at[c, to, :, :, :, cols(h)], near.at[c, q - 1, :, :, :, cols(h)],
            x_send.at[c, h, q - 1], x_recv.at[c, h, q - 1], (layer, at(zh, zl, to)),
        )

    def add_low(c, h, q):
        to = lax.rem(zl + q, lo)
        return remote(
            later.at[c, 0, to, :, :, cols(h)], low_in.at[c, q - 1, :, :, cols(h)],
            low_send.at[c, h, q - 1], low_recv.at[c, h, q - 1], (layer, at(zh, to, x)),
        )

    def add_high(c, h, q):
        to = lax.rem(zh + q, hi)
        return remote(
            later.at[c, 0, zl, to, :, cols(h)], high_in.at[c, q - 1, :, cols(h)],
            high_send.at[c, h, q - 1], high_recv.at[c, h, q - 1], (layer, at(to, zl, x)),
        )

    def give_z(c, h, q, owner):
        spot = gath.at[c, x, owner // hi, lax.rem(owner, hi), :, cols(h)]
        to = lax.rem(mine + q, deep)
        return remote(
            spot, spot, gz_send.at[c, h, q - 1], gz_recv.at[c, h, q - 1], (layer, at(lax.rem(to, hi), to // hi, x))
        )

    def give_x(c, h, q, owner):
        spot = gath.at[c, owner, :, :, :, cols(h)]
        return remote(
            spot, spot, gx_send.at[c, h, q - 1], gx_recv.at[c, h, q - 1], (layer, at(zh, zl, x + q))
        )

    def down(c, h, q):
        owner = lax.rem(x + m - q, m)
        return remote(
            gath.at[c, owner, :, :, :, cols(h)], foll.at[c, owner, :, :, :, cols(h)],
            down_send.at[c, h, q], down_recv.at[c, h, q], (below, me),
        )

    def encode(c, t):
        lhs = acts[c].reshape(block, width)
        pre = jnp.dot(lhs, enc[:, feats(t)], preferred_element_type=jnp.float32)
        pre = pre + enc_bias_ref[:, feats(t)]
        shrunk = jnp.exp2(jnp.abs(pre) * (-4.0 * math.log2(math.e)))
        grown = 1.0 + shrunk
        part = 1.0 / grown
        lost = shrunk - (grown - 1.0)
        soft = jnp.log2(grown) * (0.25 * math.log(2.0)) + lost * (part * 0.25)
        latent[:, feats(t)] = (jnp.maximum(pre, 0.0) + soft).astype(jnp.bfloat16)
        deriv[c, :, feats(t)] = jnp.where(pre >= 0.0, part, shrunk * part).astype(jnp.bfloat16)

    def decode_later(c, d):
        value = jnp.dot(latent[...], dec[1, :, dots(d)], preferred_element_type=jnp.float32)
        later[c, :, :, :, :, dots(d)] = value.astype(jnp.bfloat16).reshape(m, lo, hi, rows, dot)

        @pl.when(layer < layers - 1)
        def _():
            for h in range(d * PIECES // DOTS, (d + 1) * PIECES // DOTS):
                up(c, h).start()

    def decode_own(c, d):
        own[:, dots(d)] = jnp.dot(
            latent[...], dec[0, :, dots(d)], preferred_element_type=jnp.float32
        )

    def send_x(c, h):
        @pl.when(layer > 0)
        def _():
            up(c, h).wait_recv()

        carried = jnp.where(layer > 0, arrived[c, :, :, :, :, cols(h)].reshape(block, wide).astype(jnp.float32), 0.0)
        both = (own[:, cols(h)] + carried).astype(jnp.bfloat16)
        sums[c, :, :, :, :, cols(h)] = both.reshape(m, lo, hi, rows, wide)
        for q in range(1, m):
            add_x(c, h, q).start()

    def send_low(c, h):
        value = sums[c, x, :, :, :, cols(h)].astype(jnp.float32)
        for q in range(1, m):
            add_x(c, h, q).wait_recv()
            value = value + near[c, q - 1, :, :, :, cols(h)].astype(jnp.float32)

        @pl.when(layer < layers - 1)
        def _():
            up(c, h).wait_send()

        later[c, 0, :, :, :, cols(h)] = value.astype(jnp.bfloat16)
        for q in range(1, lo):
            add_low(c, h, q).start()

    def own_low(c, h, spot):
        value = sums[c, x, zl, spot, :, cols(h)].astype(jnp.float32)
        for q in range(1, m):
            value = value + near[c, q - 1, zl, spot, :, cols(h)].astype(jnp.float32)
        for q in range(1, lo):
            value = value + low_in[c, q - 1, spot, :, cols(h)].astype(jnp.float32)
        return value

    def send_high(c, h):
        for q in range(1, lo):
            add_low(c, h, q).wait_recv()
        for q in range(1, hi):
            to = lax.rem(zh + q, hi)
            later[c, 0, zl, to, :, cols(h)] = own_low(c, h, to).astype(jnp.bfloat16)
            add_high(c, h, q).start()

    def send_errors(c, h):
        value = own_low(c, h, zh)
        for q in range(1, hi):
            add_high(c, h, q).wait_recv()
            value = value + high_in[c, q - 1, :, cols(h)].astype(jnp.float32)
        errors = value + bias_ref[:, cols(h)] - targets_ref[c, :, cols(h)].astype(jnp.float32)
        errors_ref[c, :, cols(h)] = errors
        gath[c, x, zl, zh, :, cols(h)] = errors.astype(jnp.bfloat16)
        for q in range(1, deep):
            give_z(c, h, q, mine).start()

    def pass_x(c, h):
        for q in range(1, deep):
            give_z(c, h, q, lax.rem(mine + deep - q, deep)).wait_recv()
        for q in range(1, m):
            give_x(c, h, q, x).start()

        @pl.when(layer > 0)
        def _():
            down(c, h, 0).start()

    def pass_down(c, h):
        for q in range(1, m):
            give_x(c, h, q, lax.rem(x + m - q, m)).wait_recv()

        @pl.when(layer > 0)
        def _():
            for q in range(1, m):
                down(c, h, q).start()

    def contribute(c, t):
        own[:, :tile] = contract_width(gath[c].reshape(block, width), dec[0, feats(t), :])

    def gradient(c, t):
        if t == 0:
            @pl.when(layer < layers - 1)
            def _():
                for h in range(PIECES):
                    for q in range(m):
                        down(c, h, q).wait_recv()

            grad = own[:, :tile]
        else:
            grad = contract_width(gath[c].reshape(block, width), dec[0, feats(t), :])
        grad = grad + contract_width(foll[c].reshape(block, width), dec[1, feats(t), :])
        latent[:, feats(t)] = (grad * deriv[c, :, feats(t)].astype(jnp.float32)).astype(jnp.bfloat16)

    def weigh(c, t):
        value = lax.dot_general(
            acts[c].reshape(block, width), latent[:, feats(t)], (((0,), (0,)), ((), ())),
            preferred_element_type=jnp.float32,
        )
        if c > 0:
            value = total[:, feats(t)] + value
        if c < chunks - 1:
            total[:, feats(t)] = value
        else:
            enc[:, feats(t)] = (value * scale).astype(jnp.bfloat16)

    run = {
        "x": send_x, "low": send_low, "high": send_high, "give_z": send_errors,
        "give_x": pass_x, "down": pass_down, "contribute": contribute, "gradient": gradient, "weigh": weigh,
    }
    inside, rest = plan(chunks, tiles)

    def every(c):
        return [load_acts(c, q, l) for q in range(m) for l in range(lo)]

    small = [
        pltpu.make_async_copy(source, place, small_sem.at[i])
        for i, (source, place) in enumerate(
            ((enc_bias_hbm, enc_bias_ref), (targets_hbm, targets_ref), (bias_hbm, bias_ref))
        )
    ]
    for copy in every(0):
        copy.start()
    small[0].start()
    for t in range(tiles):
        load_enc(t).start()

    @pl.when(layer == layers - 1)
    def _():
        foll[...] = jnp.zeros_like(foll)

    barrier = pltpu.get_barrier_semaphore()
    for to in (
        [(layer, at(zh, zl, x + q)) for q in range(1, m)]
        + [(layer, at(lax.rem(mine + q, hi), lax.rem(mine + q, deep) // hi, x)) for q in range(1, deep)]
        + [(above, me), (below, me)]
    ):
        pl.semaphore_signal(barrier, inc=1, device_id=to, device_id_type=MESH)

    for copy in every(0):
        copy.wait()
    small[0].wait()
    load_enc(0).wait()
    for i in range(slots):
        load_dec(i).start()
    for copy in small[1:]:
        copy.start()
    for c in range(1, chunks):
        for copy in every(c):
            copy.start()

    def split_dec(i):
        load_dec(i).wait()
        dec[:, pl.ds(pl.multiple_of(i * raws, raws), raws), :] = jnp.transpose(raw[lax.rem(i, slots)], (1, 0, 2))

        @pl.when(i + slots < parts)
        def _():
            load_dec(i + slots).start()

    encode(0, 0)
    pl.loop(0, slots)(split_dec)
    for t in range(1, tiles):
        load_enc(t).wait()
        encode(0, t)
    pl.loop(slots, parts)(split_dec)

    for copy in small[1:]:
        copy.wait()
    for c in range(1, chunks):
        for copy in every(c):
            copy.wait()

    pl.semaphore_wait(barrier, m + deep)

    @pl.loop(0, chunks)
    def _(c):
        def attend(spot):
            for back, stage, h in inside[spot]:
                @pl.when(c >= back)
                def _():
                    run[stage](c - back, h)

        decode_later(c, 0)
        attend(0)
        decode_later(c, 1)
        attend(1)
        decode_own(c, 0)
        attend(2)
        decode_own(c, 1)
        attend(3)

        @pl.when(c < chunks - 1)
        def _():
            for t in range(tiles):
                encode(c + 1, t)
                if t < 2:
                    attend(4 + t)

    for stage, c, k in rest:
        run[stage](c, k)

    @pl.loop(0, chunks)
    def _(c):
        for h in range(PIECES):
            for q in range(1, m):
                add_x(c, h, q).wait_send()
                give_x(c, h, q, x).wait_send()
            for q in range(1, lo):
                add_low(c, h, q).wait_send()
            for q in range(1, hi):
                add_high(c, h, q).wait_send()
            for q in range(1, deep):
                give_z(c, h, q, mine).wait_send()

            @pl.when(layer > 0)
            def _():
                for q in range(m):
                    down(c, h, q).wait_send()


def step(layers, tokens, acts, enc, dec, enc_bias, targets, bias):
    hi, lo, m, chunks, rows, width = acts.shape
    features = enc.shape[1]
    block = tokens // chunks
    half, full = jnp.bfloat16, jnp.float32
    vmem = pl.BlockSpec(memory_space=pltpu.VMEM)
    outside = pl.BlockSpec(memory_space=pltpu.HBM)
    dma = pltpu.SemaphoreType.DMA
    raws = 256
    parts = features // raws
    slots = -(-parts // 2)
    pairs = [(), (m - 1,), (lo - 1,), (hi - 1,), (lo * hi - 1,), (m - 1,), (m,)]
    return pl.pallas_call(
        functools.partial(step_kernel, layers, m, lo, hi, tokens ** (-0.5)),
        out_shape=(
            jax.ShapeDtypeStruct((chunks, rows, width), full),
            jax.ShapeDtypeStruct((width, features), half),
        ),
        in_specs=[outside] * 6,
        out_specs=(vmem, vmem),
        scratch_shapes=[
            pltpu.VMEM(enc_bias.shape, full),
            pltpu.VMEM(targets.shape, half),
            pltpu.VMEM(bias.shape, full),
            pltpu.VMEM((chunks, m, lo, hi, rows, width), half),
            pltpu.VMEM((slots, raws, 2, width), half),
            pltpu.VMEM((2, features, width), half),
            pltpu.VMEM((chunks, block, features), half),
            pltpu.VMEM((block, features), half),
            pltpu.VMEM((block, max(width, tile_of(features))), full),
            pltpu.VMEM((width, features), full),
            pltpu.VMEM((chunks, m, lo, hi, rows, width), half),
            pltpu.VMEM((chunks, m, lo, hi, rows, width), half),
            pltpu.VMEM((chunks, m, lo, hi, rows, width), half),
            pltpu.VMEM((chunks, m - 1, lo, hi, rows, width), half),
            pltpu.VMEM((chunks, lo - 1, hi, rows, width), half),
            pltpu.VMEM((chunks, hi - 1, rows, width), half),
            pltpu.VMEM((chunks, m, lo, hi, rows, width), half),
            pltpu.VMEM((chunks, m, lo, hi, rows, width), half),
            dma((3,)),
            dma((chunks, m, lo)),
            dma((features // tile_of(features),)),
            dma((parts,)),
            *[dma((chunks, PIECES, *p)) for p in pairs for _ in range(2)],
        ],
        compiler_params=pltpu.CompilerParams(
            collective_id=0, has_side_effects=True, vmem_limit_bytes=46 * 2**20
        ),
        name="step",
    )(*[pltpu.with_memory_space_constraint(a, pltpu.HBM) for a in (acts, enc, dec, enc_bias, targets, bias)])


def local(layers, n, acts, targets, enc_weight, enc_bias, dec_weight, dec_bias):
    tokens, width = acts.shape[1:]
    m = inner_of(n)
    lo = inner_of(n // m)
    rows = tokens // n
    chunks = chunks_of(rows)
    errors, enc_grad = step(
        layers, tokens,
        acts.reshape(n // (m * lo), lo, m, chunks, rows // chunks, width),
        enc_weight[0], dec_weight[0], enc_bias,
        targets.reshape(chunks, rows // chunks, width), dec_bias,
    )
    return (errors.reshape(1, rows, width), enc_grad[None])


def solution(mesh):
    return jax.shard_map(
        functools.partial(local, mesh.shape["layer"], mesh.shape["feat"]),
        mesh=mesh,
        in_specs=(
            P("layer", None, None),
            P("layer", "feat", None),
            P("layer", None, "feat"),
            P("layer", "feat"),
            P("layer", "feat", None, None),
            P("layer", None),
        ),
        out_specs=(P("layer", "feat", None), P("layer", None, "feat")),
        check_vma=False,
    )
```
